128 devices in a mesh: chain: 4 (over z_hi, core), gx: 32 (over y, z_lo, x).
Axes of the slice: x: 4, y: 4, z: 4 (z_hi: 2, z_lo: 2; z = z_hi * 2 + z_lo), core: 2. Of those that a mesh axis runs over, the one named last changes fastest.
Arguments:
- position: float32 [8, 256, 16, 1024], P('chain', 'gx'), may hold values from -6 to 6
- momentum_draw: float32 [8, 256, 16, 1024], P('chain', 'gx'), may hold values from -6 to 6
- viscosity: float32 [256, 16, 1024], P('gx'), may hold values from 0.3 to 3
- observed: float32 [256, 16, 1024], P('gx'), may hold values from -18 to 18
Outputs:
- new_position: float32 [8, 256, 16, 1024], P('chain', 'gx')
- new_momentum: float32 [8, 256, 16, 1024], P('chain', 'gx')
- energies: float32 [2, 8], P(None, 'chain')
The draws below stay inside these ranges and needn't reach their ends.
All inputs are finite; a program needn't handle non-finite values.
Results may differ from the reference program's by a relative error of at most 0.00002.
Values sent between devices are 32-bit elements; how exact they have to be, the bound alone decides.
No kernel may reach another device: no remote copies, remote signals or barrier semaphores. Data moves between devices by JAX's collectives and lax.ppermute only.
A program may use at most 64 MiB of HBM per device.

```python
import math
import jax
import jax.numpy as jnp
from jax import lax

NZ = 16
NY = 1024
LEAPS = 2
CHAINS = 8
NX = 256


def draw_observed(key, part):
    rows = jnp.arange(NX, dtype=jnp.float32) / NX
    growth = 1.0 + 2.0 * rows
    base = 2.0 * jax.random.truncated_normal(key, -3.0, 3.0, (NX, NZ, NY), jnp.float32)
    return base * growth[:, None, None]


def block_levels(own_key, dims, shards, least, high):
    factor_of = 1.0
    for axis_at, blocks in shards:
        heights = jax.random.uniform(jax.random.fold_in(jax.random.fold_in(own_key, 6), axis_at), (blocks,), jnp.float32, least / len(shards), high / len(shards))
        factor_of = factor_of * jnp.repeat(jnp.exp(heights), dims[axis_at] // blocks).reshape((-1,) + (1,) * (len(dims) - 1 - axis_at))
    return factor_of


def bell_draw(stream_key, dims, deviation, reach, shards=(), kind=jnp.bfloat16):
    entries = deviation * jax.random.normal(stream_key, dims, jnp.float32)
    if shards:
        entries = entries * block_levels(stream_key, dims, shards, -0.22, 0.18)
    return jnp.clip(entries, -reach, reach).astype(kind)


def setup_inputs(seed: int = 0) -> dict:
    splits = jax.random.split(jax.random.key(seed), 5)
    return {
        "position": bell_draw(splits[0], (CHAINS, NX, NZ, NY), 1.0, 6.0, ((0, 4), (1, 32)), jnp.float32),
        "momentum_draw": bell_draw(splits[1], (CHAINS, NX, NZ, NY), 1.0, 6.0, ((0, 4), (1, 32)), jnp.float32),
        "viscosity": jnp.clip(jnp.exp(math.log(3.0) - 2.3025851 * jax.random.uniform(splits[2], (NX, NZ, NY), jnp.float32) ** block_levels(splits[2], (NX, NZ, NY), ((0, 32),), -0.2, 0.2)), 0.3, 3.0),
        "observed": draw_observed(jax.random.fold_in(splits[4], 71), 0),
    }


stencil_weights = (4.0, -0.3, -0.1, -0.05)
inv_noise = 0.25
prior_weight = 0.5
step_size = 0.05

def apply_kernel(extended):
    lead = extended.ndim - 3
    padded = jnp.pad(extended, ((0, 0),) * lead + ((0, 0), (1, 1), (1, 1)))
    planes = extended.shape[lead] - 2
    depth_cells = extended.shape[lead + 1]
    across = extended.shape[lead + 2]
    summed = jnp.zeros(extended.shape[:lead] + (planes, depth_cells, across), jnp.float32)
    for shift_x in range(3):
        for shift_z in range(3):
            for shift_y in range(3):
                order = abs(shift_x - 1) + abs(shift_z - 1) + abs(shift_y - 1)
                summed = summed + stencil_weights[order] * padded[..., shift_x:shift_x + planes, shift_z:shift_z + depth_cells, shift_y:shift_y + across]
    return summed

def wrap_planes(source):
    return jnp.concatenate([source[-1:], source, source[:1]], axis=0)

def chain_gradient(source, viscosity, observed):
    misfit = viscosity * apply_kernel(wrap_planes(source)) - observed
    scaled = viscosity * misfit
    return (inv_noise * apply_kernel(wrap_planes(scaled)) + prior_weight * source, misfit)

def chain_energy(source, misfit, moment, inverse_mass):
    potential = 0.5 * inv_noise * jnp.sum(misfit * misfit) + 0.5 * prior_weight * jnp.sum(source * source)
    kinetic = 0.5 * jnp.sum(inverse_mass * moment * moment)
    return potential + kinetic

def reference(position, momentum_draw, viscosity, observed):
    first = lax.optimization_barrier(jnp.sum(position, axis=0))
    second = lax.optimization_barrier(jnp.sum(position * position, axis=0))
    mean_value = first / CHAINS
    inverse_mass = 0.5 + second / CHAINS - mean_value * mean_value
    cells = NX * NZ * NY

    def one_chain(pair):
        source, draw_value = pair
        moment = draw_value / jnp.sqrt(inverse_mass)
        slope, misfit = chain_gradient(source, viscosity, observed)
        start_value = chain_energy(source, misfit, moment, inverse_mass) / cells
        for leap in range(LEAPS):
            moment = moment - 0.5 * step_size * slope
            source = source + step_size * inverse_mass * moment
            slope, misfit = chain_gradient(source, viscosity, observed)
            moment = moment - 0.5 * step_size * slope
        end_value = chain_energy(source, misfit, moment, inverse_mass) / cells
        return (source, moment, jnp.stack([start_value, end_value]))
    new_position, new_momentum, energy_rows = lax.map(one_chain, (position, momentum_draw))
    return (new_position, new_momentum, jnp.transpose(energy_rows))
```

```python
import jax
import jax.numpy as jnp
from jax import lax
from jax.sharding import PartitionSpec as P

LEAPS = 2


stencil_weights = (4.0, -0.3, -0.1, -0.05)
inv_noise = 0.25
prior_weight = 0.5
step_size = 0.05


def with_halo(block, sides, width):
    for axis, dim in sides:
        count = lax.axis_size(axis)
        forward = [(i, i + 1) for i in range(count - 1)]
        forward.append((count - 1, 0))
        backward = [(target, source) for source, target in forward]
        low = lax.ppermute(
            lax.slice_in_dim(block, block.shape[dim] - width, None, axis=dim), axis, forward
        )
        high = lax.ppermute(lax.slice_in_dim(block, 0, width, axis=dim), axis, backward)
        block = jnp.concatenate([low, block, high], axis=dim)
    return block


def apply_kernel(extended):
    lead = extended.ndim - 3
    padded = jnp.pad(extended, ((0, 0),) * lead + ((0, 0), (1, 1), (1, 1)))
    planes = extended.shape[lead] - 2
    depth_cells = extended.shape[lead + 1]
    across = extended.shape[lead + 2]
    summed = jnp.zeros(extended.shape[:lead] + (planes, depth_cells, across), jnp.float32)
    for shift_x in range(3):
        for shift_z in range(3):
            for shift_y in range(3):
                order = abs(shift_x - 1) + abs(shift_z - 1) + abs(shift_y - 1)
                summed = (
                    summed
                    + stencil_weights[order]
                    * padded[
                        ...,
                        shift_x : shift_x + planes,
                        shift_z : shift_z + depth_cells,
                        shift_y : shift_y + across,
                    ]
                )
    return summed


def gradient_narrow(source, viscosity, observed):
    extended = with_halo(source, (("gx", 1),), 1)
    misfit = viscosity * apply_kernel(extended) - observed
    scaled = viscosity * misfit
    rims = with_halo(scaled, (("gx", 1),), 1)
    return (inv_noise * apply_kernel(rims) + prior_weight * source, misfit)


def local_sums(source, misfit, moment, inverse_mass):
    potential = 0.5 * inv_noise * jnp.sum(
        misfit * misfit, axis=(1, 2, 3)
    ) + 0.5 * prior_weight * jnp.sum(source * source, axis=(1, 2, 3))
    kinetic = 0.5 * jnp.sum(inverse_mass * moment * moment, axis=(1, 2, 3))
    return (potential, kinetic)


def chain_inverse_mass(position, chain_count):
    count = lax.axis_size("chain")
    near = [(i, i ^ 1) for i in range(count)]
    far = [(i, i ^ 2) for i in range(count)]
    sums = jnp.stack([jnp.sum(position, axis=0), jnp.sum(position * position, axis=0)], axis=1)
    half = sums.shape[0] // 2
    core = lax.axis_index("chain") % 2
    keep = lax.dynamic_slice_in_dim(sums, half * core, half, 0)
    send = lax.dynamic_slice_in_dim(sums, half * (1 - core), half, 0)
    part = keep + lax.ppermute(send, "chain", near)
    part = part + lax.ppermute(part, "chain", far)
    mean_value = part[:, 0] / chain_count
    mine = 0.5 + part[:, 1] / chain_count - mean_value * mean_value
    other = lax.ppermute(mine, "chain", near)
    return jnp.concatenate(
        [jnp.where(core == 0, mine, other), jnp.where(core == 0, other, mine)], axis=0
    )


def slab_total(parts):
    count = lax.axis_size("gx")
    row = jnp.pad(parts.reshape(1, -1), ((0, 0), (0, 128 - parts.size)))
    rows = lax.all_to_all(jnp.broadcast_to(row, (count, 128)), "gx", 0, 0, tiled=True)
    return jnp.sum(rows, axis=0)[: parts.size].reshape(parts.shape)


def local(position, momentum_draw, viscosity, observed):
    chain_count = position.shape[0] * lax.axis_size("chain")
    cells = position.shape[1] * lax.axis_size("gx") * position.shape[2] * position.shape[3]
    inverse_mass = chain_inverse_mass(position, chain_count)

    def gradient(source):
        return gradient_narrow(source, viscosity, observed)

    moment = momentum_draw / jnp.sqrt(inverse_mass)
    source = position
    slope, misfit = gradient(source)
    start_potential, start_kinetic = local_sums(source, misfit, moment, inverse_mass)
    for leap in range(LEAPS):
        moment = moment - 0.5 * step_size * slope
        source = source + step_size * inverse_mass * moment
        slope, misfit = gradient(source)
        moment = moment - 0.5 * step_size * slope
    end_potential, end_kinetic = local_sums(source, misfit, moment, inverse_mass)
    energies = slab_total(
        jnp.stack([start_potential + start_kinetic, end_potential + end_kinetic])
    ) / cells
    return (source, moment, energies)


def solution(mesh):
    in_specs = (
        P("chain", "gx", None, None),
        P("chain", "gx", None, None),
        P("gx", None, None),
        P("gx", None, None),
    )
    out_specs = (P("chain", "gx", None, None), P("chain", "gx", None, None), P(None, "chain"))
    return jax.shard_map(local, mesh=mesh, in_specs=in_specs, out_specs=out_specs, check_vma=False)
```

```python
import jax
import jax.numpy as jnp
from jax import lax
from jax.experimental import pallas as pl
from jax.experimental.pallas import tpu as pltpu
from jax.sharding import PartitionSpec as P

LEAPS = 2

unit = -0.05
inv_noise = 0.25
prior_weight = 0.5
step_size = 0.05
LANES = 128
WIDE = 2


def call(kernel, out_shapes, scratch, name, work):
    spec = pl.BlockSpec(memory_space=pltpu.VMEM)
    return pl.pallas_call(
        kernel,
        out_shape=[jax.ShapeDtypeStruct(shape, jnp.float32) for shape in out_shapes],
        out_specs=[spec] * len(out_shapes),
        scratch_shapes=[pltpu.VMEM(shape, jnp.float32) for shape in scratch],
        compiler_params=pltpu.CompilerParams(vmem_limit_bytes=32 << 20),
        cost_estimate=pl.CostEstimate(flops=work, bytes_accessed=work // 8, transcendentals=0),
        name=name,
    )


def tiles(width):
    return [slice(j * LANES, (j + 1) * LANES) for j in range(width // LANES)]


def depth_sum(v):
    depth = v.shape[0]
    row = lax.broadcasted_iota(jnp.int32, v.shape, 0)
    below = jnp.where(row == 0, 0.0, pltpu.roll(v, 1, 0))
    above = jnp.where(row == depth - 1, 0.0, pltpu.roll(v, depth - 1, 0))
    return below + above


def stencil_plane(field, deep, chain, plane):
    cuts = tiles(field.shape[-1])
    edge_terms, own_terms = [], []
    for cut in cuts:
        v = field[chain, plane, :, cut]
        w = deep[chain, plane, :, cut] + (
            field[chain, plane - 1, :, cut] + field[chain, plane + 1, :, cut]
        )
        corner = deep[chain, plane - 1, :, cut] + deep[chain, plane + 1, :, cut]
        t = 6.0 * v + (2.0 * w + corner)
        d = t + w
        edge_terms.append(t)
        own_terms.append((d + d) - 92.0 * v)
    lane = lax.broadcasted_iota(jnp.int32, edge_terms[0].shape, 1)
    ups = [pltpu.roll(t, 1, 1) for t in edge_terms]
    downs = [pltpu.roll(t, LANES - 1, 1) for t in edge_terms]
    result = []
    for j in range(len(cuts)):
        before = ups[j - 1] if j else 0.0
        after = downs[j + 1] if j + 1 < len(cuts) else 0.0
        left = jnp.where(lane == 0, before, ups[j])
        right = jnp.where(lane == LANES - 1, after, downs[j])
        result.append(own_terms[j] + (left + right))
    return list(zip(cuts, result, strict=True))


def fill(field, deep, chain, target, source, index):
    for cut in tiles(field.shape[-1]):
        v = source[index + (slice(None), cut)]
        field[chain, target, :, cut] = v
        deep[chain, target, :, cut] = depth_sum(v)


def extend(q, low, high, field, deep):
    chains, planes = q.shape[:2]
    for chain in range(chains):
        for i in range(WIDE):
            fill(field, deep, chain, i, low, (chain * WIDE + i,))
            fill(field, deep, chain, WIDE + planes + i, high, (chain * WIDE + i,))

        def body(x, carry, chain=chain):
            fill(field, deep, chain, WIDE + x, q, (chain, x))
            return carry

        lax.fori_loop(0, planes, body, 0)


def weigh(field, deep, viscous, target, scaled, scaled_deep, want):
    chains, planes = field.shape[0], field.shape[1] - 2 * WIDE
    totals = []
    for chain in range(chains):

        def plane(x, total, chain=chain):
            for cut, k in stencil_plane(field, deep, chain, x + 1):
                nu = viscous[x, :, cut]
                misfit = (unit * nu) * k - target[x, :, cut]
                s = nu * misfit
                scaled[chain, x, :, cut] = s
                scaled_deep[chain, x, :, cut] = depth_sum(s)
                if total is not None:
                    total = total + misfit * misfit
            return total

        def rim(i, carry, plane=plane):
            plane(i * (planes + 1), None)
            return carry

        lax.fori_loop(0, 2, rim, 0)
        if want:
            zero = jnp.zeros((field.shape[2], LANES), jnp.float32)
            totals.append(lax.fori_loop(1, planes + 1, plane, zero))
        else:

            def quiet(x, carry, plane=plane):
                plane(x, None)
                return carry

            lax.fori_loop(1, planes + 1, quiet, 0)
    return totals


def fold(total):
    return total[:8] + total[8:]


def start_kernel(q, nu, obs, keep, send, to_high, to_low):
    core = lax.rem(lax.axis_index("chain"), 2)
    chains, planes = q.shape[:2]
    half = planes // 2

    def body(x, carry):
        for out, base in ((keep, core * half), (send, (1 - core) * half)):
            for cut in tiles(q.shape[-1]):
                first = q[0, base + x, :, cut]
                second = first * first
                for chain in range(1, chains):
                    v = q[chain, base + x, :, cut]
                    first = first + v
                    second = second + v * v
                out[x, 0, :, cut] = first
                out[x, 1, :, cut] = second
        return carry

    lax.fori_loop(0, half, body, 0)
    for chain in range(chains):
        for i in range(WIDE):
            to_high[chain * WIDE + i] = q[chain, planes - WIDE + i]
            to_low[chain * WIDE + i] = q[chain, i]
    to_high[chains * WIDE] = nu[planes - 1]
    to_low[chains * WIDE] = nu[0]
    to_high[chains * WIDE + 1] = obs[planes - 1]
    to_low[chains * WIDE + 1] = obs[0]


def first_kernel(q, low, high, nu, obs, slope, nu_wide, obs_wide, potential, field, deep, scaled, scaled_deep):
    chains, planes = q.shape[:2]
    for wide, own, at in ((nu_wide, nu, chains * WIDE), (obs_wide, obs, chains * WIDE + 1)):
        wide[0] = low[at]
        wide[planes + 1] = high[at]

        def body(x, carry, wide=wide, own=own):
            wide[x + 1] = own[x]
            return carry

        lax.fori_loop(0, planes, body, 0)
    extend(q, low, high, field, deep)
    misfits = weigh(field, deep, nu_wide, obs_wide, scaled, scaled_deep, True)
    for chain in range(chains):

        def body(x, total, chain=chain):
            for cut, k in stencil_plane(scaled, scaled_deep, chain, x + 1):
                v = q[chain, x, :, cut]
                slope[chain, x, :, cut] = (inv_noise * unit) * k + prior_weight * v
                total = total + v * v
            return total

        squares = lax.fori_loop(0, planes, body, jnp.zeros_like(misfits[chain]))
        potential[chain] = fold(
            (0.5 * inv_noise) * misfits[chain] + (0.5 * prior_weight) * squares
        )


def add_kernel(a, b, out):
    def body(x, carry):
        out[x] = a[x] + b[x]
        return carry

    lax.fori_loop(0, a.shape[0], body, 0)


def mass_kernel(count, a, b, out):
    def body(x, carry):
        mean = (a[x, 0] + b[x, 0]) / count
        out[x] = 0.5 + (a[x, 1] + b[x, 1]) / count - mean * mean
        return carry

    lax.fori_loop(0, a.shape[0], body, 0)


def launch_kernel(q, draw, slope, mine, other, new_q, new_p, mass, kinetic, to_high, to_low):
    core = lax.rem(lax.axis_index("chain"), 2)
    chains, planes = q.shape[:2]
    half = planes // 2
    totals = [jnp.zeros((q.shape[2], LANES), jnp.float32)] * chains
    for part, base in ((mine, core * half), (other, (1 - core) * half)):

        def body(i, totals, part=part, base=base):
            x = base + i
            totals = list(totals)
            for cut in tiles(q.shape[-1]):
                im = part[i, :, cut]
                mass[x, :, cut] = im
                inverse_root = 1.0 / jnp.sqrt(im)
                for chain in range(chains):
                    p = draw[chain, x, :, cut] * inverse_root
                    totals[chain] = totals[chain] + im * p * p
                    p = p - (0.5 * step_size) * slope[chain, x, :, cut]
                    new_p[chain, x, :, cut] = p
                    new_q[chain, x, :, cut] = q[chain, x, :, cut] + step_size * im * p
            return tuple(totals)

        totals = lax.fori_loop(0, half, body, tuple(totals))
    for chain in range(chains):
        kinetic[chain] = fold(0.5 * totals[chain])
        for i in range(WIDE):
            to_high[chain * WIDE + i] = new_q[chain, planes - WIDE + i]
            to_low[chain * WIDE + i] = new_q[chain, i]


def leap_kernel(q, low, high, nu, obs, p, mass, new_q, new_p, to_high, to_low, field, deep, scaled, scaled_deep):
    chains, planes = q.shape[:2]
    extend(q, low, high, field, deep)
    weigh(field, deep, nu, obs, scaled, scaled_deep, False)
    for chain in range(chains):

        def body(x, carry, chain=chain):
            for cut, k in stencil_plane(scaled, scaled_deep, chain, x + 1):
                v = q[chain, x, :, cut]
                slope = (inv_noise * unit) * k + prior_weight * v
                moment = p[chain, x, :, cut] - step_size * slope
                new_p[chain, x, :, cut] = moment
                new_q[chain, x, :, cut] = v + step_size * mass[x, :, cut] * moment
            return carry

        lax.fori_loop(0, planes, body, 0)
        for i in range(WIDE):
            to_high[chain * WIDE + i] = new_q[chain, planes - WIDE + i]
            to_low[chain * WIDE + i] = new_q[chain, i]


def last_kernel(q, low, high, nu, obs, p, mass, potential, kinetic, new_p, rows, field, deep, scaled, scaled_deep):
    chains, planes = q.shape[:2]
    extend(q, low, high, field, deep)
    misfits = weigh(field, deep, nu, obs, scaled, scaled_deep, True)
    sub = lax.broadcasted_iota(jnp.int32, (8, LANES), 0)
    lane = lax.broadcasted_iota(jnp.int32, (8, LANES), 1)
    mark = jnp.zeros((8, LANES), jnp.float32)
    for chain in range(chains):

        def body(x, total, chain=chain):
            for cut, k in stencil_plane(scaled, scaled_deep, chain, x + 1):
                v = q[chain, x, :, cut]
                slope = (inv_noise * unit) * k + prior_weight * v
                moment = p[chain, x, :, cut] - (0.5 * step_size) * slope
                new_p[chain, x, :, cut] = moment
                total = total + (
                    (0.5 * prior_weight) * (v * v) + (0.5 * mass[x, :, cut]) * (moment * moment)
                )
            return total

        rest = lax.fori_loop(0, planes, body, jnp.zeros_like(misfits[chain]))
        end = fold((0.5 * inv_noise) * misfits[chain] + rest)
        start = potential[chain] + kinetic[chain]
        for row, tile in enumerate((start, end)):
            mark = jnp.where((sub == row) & (lane == chain), jnp.sum(tile), mark)
    for i in range(rows.shape[0]):
        rows[i] = mark


def local(position, momentum_draw, viscosity, observed):
    chains, planes, depth, across = position.shape
    groups, slabs = lax.axis_size("chain"), lax.axis_size("gx")
    cells = planes * slabs * depth * across
    near = [(i, i ^ 1) for i in range(groups)]
    far = [(i, i ^ 2) for i in range(groups)]
    forward = [(i, (i + 1) % slabs) for i in range(slabs)]
    backward = [(i, (i - 1) % slabs) for i in range(slabs)]
    half = planes // 2
    block, plane = (chains, planes, depth, across), (depth, across)
    rim = (chains * WIDE, *plane)
    wide = (planes + 2, *plane)
    field = (chains, planes + 2 * WIDE, *plane)
    scaled = (chains, *wide)
    scratch = [field, field, scaled, scaled]
    sums = (half, 2, *plane)
    tile = (chains, 8, LANES)
    cells_here = chains * planes * depth * across

    keep, send, to_high, to_low = call(
        start_kernel, [sums, sums, (chains * WIDE + 2, *plane), (chains * WIDE + 2, *plane)], [], "start", cells_here * 4
    )(position, viscosity, observed)
    part = call(add_kernel, [sums], [], "add", cells_here)(keep, lax.ppermute(send, "chain", near))[0]
    far_part = lax.ppermute(part, "chain", far)
    low = lax.ppermute(to_high, "gx", forward)
    high = lax.ppermute(to_low, "gx", backward)
    slope, nu, obs, potential = call(
        first_kernel, [block, wide, wide, tile], scratch, "first", cells_here * 60
    )(position, low, high, viscosity, observed)

    def mass_body(*refs):
        mass_kernel(chains * groups, *refs)

    mine = call(mass_body, [(half, *plane)], [], "mass", cells_here)(part, far_part)[0]
    other = lax.ppermute(mine, "chain", near)
    q, p, mass, kinetic, to_high, to_low = call(
        launch_kernel, [block, block, (planes, *plane), tile, rim, rim], [], "launch", cells_here * 8
    )(position, momentum_draw, slope, mine, other)
    for _ in range(LEAPS - 1):
        low = lax.ppermute(to_high, "gx", forward)
        high = lax.ppermute(to_low, "gx", backward)
        q, p, to_high, to_low = call(
            leap_kernel, [block, block, rim, rim], scratch, "leap", cells_here * 60
        )(q, low, high, nu, obs, p, mass)
    low = lax.ppermute(to_high, "gx", forward)
    high = lax.ppermute(to_low, "gx", backward)
    p, rows = call(
        last_kernel, [block, (slabs, 8, LANES)], scratch, "last", cells_here * 60
    )(q, low, high, nu, obs, p, mass, potential, kinetic)
    rows = lax.all_to_all(rows, "gx", 0, 0, tiled=True)
    energies = jnp.sum(rows[:, :2, :chains], axis=0) / cells
    return (q, p, energies)


def solution(mesh):
    in_specs = (
        P("chain", "gx", None, None),
        P("chain", "gx", None, None),
        P("gx", None, None),
        P("gx", None, None),
    )
    out_specs = (P("chain", "gx", None, None), P("chain", "gx", None, None), P(None, "chain"))
    return jax.shard_map(local, mesh=mesh, in_specs=in_specs, out_specs=out_specs, check_vma=False)
```

```python
import jax
import jax.numpy as jnp
from jax import lax
from jax.experimental import pallas as pl
from jax.experimental.pallas import tpu as pltpu
from jax.sharding import PartitionSpec as P

LEAPS = 2

unit = -0.05
inv_noise = 0.25
prior_weight = 0.5
step_size = 0.05
LANES = 128
WIDE = 2


def call(kernel, out_shapes, scratch, name, work, ins=None):
    spec = pl.BlockSpec(memory_space=pltpu.VMEM)
    more = {} if ins is None else {"in_specs": ins}
    return pl.pallas_call(
        kernel,
        out_shape=[jax.ShapeDtypeStruct(shape, jnp.float32) for shape in out_shapes],
        out_specs=[spec] * len(out_shapes),
        scratch_shapes=[
            pltpu.VMEM(shape, jnp.float32) if isinstance(shape, tuple) else shape
            for shape in scratch
        ],
        compiler_params=pltpu.CompilerParams(vmem_limit_bytes=32 << 20),
        cost_estimate=pl.CostEstimate(flops=work, bytes_accessed=work // 8, transcendentals=0),
        name=name,
        **more,
    )


def tiles(width):
    return [slice(j * LANES, (j + 1) * LANES) for j in range(width // LANES)]


def depth_sum(v):
    depth = v.shape[0]
    row = lax.broadcasted_iota(jnp.int32, v.shape, 0)
    below = jnp.where(row == 0, 0.0, pltpu.roll(v, 1, 0))
    above = jnp.where(row == depth - 1, 0.0, pltpu.roll(v, depth - 1, 0))
    return below + above


def stencil(planes, deeps):
    cuts = tiles(planes[1].shape[-1])
    edge_terms, own_terms = [], []
    for cut in cuts:
        v = planes[1][:, cut]
        w = deeps[1][:, cut] + (planes[0][:, cut] + planes[2][:, cut])
        corner = deeps[0][:, cut] + deeps[2][:, cut]
        t = 6.0 * v + (2.0 * w + corner)
        d = t + w
        edge_terms.append(t)
        own_terms.append((d + d) - 92.0 * v)
    lane = lax.broadcasted_iota(jnp.int32, edge_terms[0].shape, 1)
    ups = [pltpu.roll(t, 1, 1) for t in edge_terms]
    downs = [pltpu.roll(t, LANES - 1, 1) for t in edge_terms]
    result = []
    for j in range(len(cuts)):
        before = ups[j - 1] if j else 0.0
        after = downs[j + 1] if j + 1 < len(cuts) else 0.0
        left = jnp.where(lane == 0, before, ups[j])
        right = jnp.where(lane == LANES - 1, after, downs[j])
        result.append(own_terms[j] + (left + right))
    return list(zip(cuts, result, strict=True))


def deepen(deep, source):
    for cut in tiles(source.shape[-1]):
        deep[:, cut] = depth_sum(source[:, cut])


def weigh(view, deep, nu, target, out, out_deep):
    total = 0.0
    for cut, k in stencil(view, deep):
        n = nu[:, cut]
        misfit = (unit * n) * k - target[:, cut]
        s = n * misfit
        out[:, cut] = s
        out_deep[:, cut] = depth_sum(s)
        total = total + misfit * misfit
    return total


def fold(total):
    return total[:8] + total[8:]


def interior(q, nu, obs, scaled, deep, scaled_deep, use):
    chains, planes = q.shape[:2]
    totals = []
    for chain in range(chains):
        for x in range(planes):
            deepen(deep.at[chain, x], q.at[chain, x])
    for chain in range(chains):
        total = 0.0
        for x in range(1, planes - 1):
            near = range(x - 1, x + 2)
            total = total + weigh(
                [q.at[chain, i] for i in near],
                [deep.at[chain, i] for i in near],
                nu.at[x],
                obs.at[x],
                scaled.at[chain, x - 1],
                scaled_deep.at[chain, x - 1],
            )
        totals.append(total)
    for chain in range(chains):
        for x in range(2, planes - 2):
            near = range(x - 2, x + 1)
            view = [scaled.at[chain, i] for i in near]
            for cut, k in stencil(view, [scaled_deep.at[chain, i] for i in near]):
                slope = (inv_noise * unit) * k + prior_weight * q[chain, x, :, cut]
                use(chain, x, cut, slope)
    return totals


def parity():
    return lax.rem(lax.axis_index("gx"), 2)


def place_halo(halo, from_a, from_b):
    odd = parity()
    chains = halo.shape[1]
    for chain in range(chains):
        for i in range(WIDE):
            halo[1 - odd, chain, i] = from_a[chain * WIDE + i]
            halo[odd, chain, i] = from_b[chain * WIDE + i]


def rims(q, halo, nu, obs, nu_halo, obs_halo, scaled, deep, rim_scaled, scaled_deep, use):
    chains, planes = q.shape[:2]

    def at(chain, x):
        if x < 0:
            return halo.at[0, chain, WIDE + x]
        if x >= planes:
            return halo.at[1, chain, x - planes]
        return q.at[chain, x]

    def scaled_at(chain, x):
        if x in (-1, 0):
            return rim_scaled.at[chain, x + 1]
        if x in (planes - 1, planes):
            return rim_scaled.at[chain, x - planes + 3]
        return scaled.at[chain, x - 1]

    sides = ((-2, -1, 0, 1), (planes + 1, planes, planes - 1, planes - 2))
    totals = []
    for chain in range(chains):
        for side in sides:
            for x in side:
                deepen(deep.at[chain, x + WIDE], at(chain, x))
    for chain in range(chains):
        total = 0.0
        for s, side in enumerate(sides):
            for x in side[1:3]:
                outer = x == side[1]
                near = range(x - 1, x + 2)
                squares = weigh(
                    [at(chain, i) for i in near],
                    [deep.at[chain, i + WIDE] for i in near],
                    nu_halo.at[s] if outer else nu.at[x],
                    obs_halo.at[s] if outer else obs.at[x],
                    scaled_at(chain, x),
                    scaled_deep.at[chain, x + 1],
                )
                total = total if outer else total + squares
            for x in (1, 2) if s == 0 else (planes - 2, planes - 3):
                deepen(scaled_deep.at[chain, x + 1], scaled_at(chain, x))
        totals.append(total)
    for chain in range(chains):
        for x in (0, 1, planes - 2, planes - 1):
            near = range(x - 1, x + 2)
            view = [scaled_at(chain, i) for i in near]
            for cut, k in stencil(view, [scaled_deep.at[chain, i + 1] for i in near]):
                slope = (inv_noise * unit) * k + prior_weight * q[chain, x, :, cut]
                use(chain, x, cut, slope)
    return totals


def fetch_kernel(q, nu, obs, to_a, to_b, sems):
    odd = parity()
    chains, planes = q.shape[:2]
    copies = []
    for out, low in ((to_a, odd), (to_b, 1 - odd)):
        start = (1 - low) * (planes - WIDE)
        edge = (1 - low) * (planes - 1)
        for chain in range(chains):
            copies.append((q.at[chain, pl.ds(start, WIDE)], out.at[pl.ds(chain * WIDE, WIDE)]))
        copies.append((nu.at[edge], out.at[chains * WIDE]))
        copies.append((obs.at[edge], out.at[chains * WIDE + 1]))
    started = [
        pltpu.make_async_copy(source, target, sems.at[i])
        for i, (source, target) in enumerate(copies)
    ]
    for copy in started:
        copy.start()
    for copy in started:
        copy.wait()


def sums_kernel(q, keep, send):
    core = lax.rem(lax.axis_index("chain"), 2)
    chains, planes = q.shape[:2]
    half = planes // 2
    for x in range(half):
        for out, base in ((keep, core * half), (send, (1 - core) * half)):
            for cut in tiles(q.shape[-1]):
                first = q[0, base + x, :, cut]
                second = first * first
                for chain in range(1, chains):
                    v = q[chain, base + x, :, cut]
                    first = first + v
                    second = second + v * v
                out[x, 0, :, cut] = first
                out[x, 1, :, cut] = second


def add_kernel(a, b, rim, inner):
    core = lax.rem(lax.axis_index("chain"), 2)
    count = rim.shape[0]
    for x in range(count):
        at = core * count + x
        rim[x] = a[at] + b[at]
        at = (1 - core) * count + x
        inner[x] = a[at] + b[at]


def mass_kernel(count, a, b, out):
    for x in range(a.shape[0]):
        mean = (a[x, 0] + b[x, 0]) / count
        out[x] = 0.5 + (a[x, 1] + b[x, 1]) / count - mean * mean


def first_inner_kernel(q, nu, obs, scaled, slope, potential, deep, scaled_deep):
    chains, planes = q.shape[:2]

    def use(chain, x, cut, value):
        slope[chain, x - 2, :, cut] = value

    misfits = interior(q, nu, obs, scaled, deep, scaled_deep, use)
    for chain in range(chains):
        squares = 0.0
        for x in range(planes):
            for cut in tiles(q.shape[-1]):
                v = q[chain, x, :, cut]
                squares = squares + v * v
        potential[chain] = fold(
            (0.5 * inv_noise) * misfits[chain] + (0.5 * prior_weight) * squares
        )


def first_rim_kernel(
    q, from_a, from_b, nu, obs, scaled, before,
    slope, nu_halo, obs_halo, potential, halo, deep, rim_scaled, scaled_deep,
):
    odd = parity()
    chains, planes = q.shape[:2]
    place_halo(halo, from_a, from_b)
    for out, at in ((nu_halo, chains * WIDE), (obs_halo, chains * WIDE + 1)):
        out[1 - odd] = from_a[at]
        out[odd] = from_b[at]

    def use(chain, x, cut, value):
        slope[chain, x if x < 2 else x - planes + 4, :, cut] = value

    misfits = rims(
        q, halo, nu, obs, nu_halo, obs_halo, scaled, deep, rim_scaled, scaled_deep, use
    )
    for chain in range(chains):
        potential[chain] = before[chain] + fold((0.5 * inv_noise) * misfits[chain])


def launch(q, draw, slope, mine, other, base, new_q, new_p, mass, totals, where_q):
    chains = q.shape[0]
    for part, (start, offset) in ((mine, base[0]), (other, base[1])):
        for i in range(part.shape[0]):
            for cut in tiles(q.shape[-1]):
                im = part[i, :, cut]
                mass[offset + i, :, cut] = im
                inverse_root = 1.0 / jnp.sqrt(im)
                for chain in range(chains):
                    p = draw[chain, start + i, :, cut] * inverse_root
                    totals[chain] = totals[chain] + im * p * p
                    p = p - (0.5 * step_size) * slope[chain, offset + i, :, cut]
                    new_p[chain, offset + i, :, cut] = p
                    new_q[chain, offset + i, :, cut] = (
                        q[chain, start + i, :, cut] + step_size * im * p
                    )


def send_rims(source, to_a, to_b):
    odd = parity()
    for chain in range(source.shape[0]):
        for i in range(WIDE):
            to_a[chain * WIDE + i] = source[chain, (1 - odd) * WIDE + i]
            to_b[chain * WIDE + i] = source[chain, odd * WIDE + i]


def launch_rim_kernel(q, draw, slope, mine, other, new_q, new_p, mass, kinetic, to_a, to_b):
    core = lax.rem(lax.axis_index("chain"), 2)
    chains, planes = q.shape[:2]
    far = planes - WIDE
    totals = [0.0] * chains
    base = ((core * far, core * WIDE), ((1 - core) * far, (1 - core) * WIDE))
    launch(q, draw, slope, mine, other, base, new_q, new_p, mass, totals, None)
    for chain in range(chains):
        kinetic[chain] = fold(0.5 * totals[chain])
    send_rims(new_q, to_a, to_b)


def launch_inner_kernel(
    q, draw, slope, mine, other, rim_q, before, new_q, new_p, mass, kinetic, own_q, own_p
):
    core = lax.rem(lax.axis_index("chain"), 2)
    chains, planes = q.shape[:2]
    half = planes // 2 - WIDE
    totals = [0.0] * chains
    base = tuple((WIDE + c * half, c * half) for c in (core, 1 - core))
    launch(q, draw, slope, mine, other, base, own_q, new_p, mass, totals, None)
    for chain in range(chains):
        kinetic[chain] = before[chain] + fold(0.5 * totals[chain])
    join(new_q, own_q, rim_q)


def join(whole, inner, rim):
    chains, planes = whole.shape[:2]
    for chain in range(chains):
        for x in range(planes):
            if x < WIDE:
                whole[chain, x] = rim[chain, x]
            elif x >= planes - WIDE:
                whole[chain, x] = rim[chain, x - planes + 2 * WIDE]
            else:
                whole[chain, x] = inner[chain, x - WIDE]


def leap_inner_kernel(q, nu, obs, p, mass, scaled, new_q, new_p, deep, scaled_deep):
    def use(chain, x, cut, slope):
        moment = p[chain, x - WIDE, :, cut] - step_size * slope
        new_p[chain, x - WIDE, :, cut] = moment
        new_q[chain, x - WIDE, :, cut] = (
            q[chain, x, :, cut] + step_size * mass[x - WIDE, :, cut] * moment
        )

    interior(q, nu, obs, scaled, deep, scaled_deep, use)


def leap_rim_kernel(
    q, from_a, from_b, nu, obs, nu_halo, obs_halo, p, mass, scaled, inner_q,
    new_q, new_p, to_a, to_b, halo, deep, rim_scaled, scaled_deep, rim_q,
):
    planes = q.shape[1]
    place_halo(halo, from_a, from_b)

    def use(chain, x, cut, slope):
        at = x if x < WIDE else x - planes + 2 * WIDE
        moment = p[chain, at, :, cut] - step_size * slope
        new_p[chain, at, :, cut] = moment
        rim_q[chain, at, :, cut] = q[chain, x, :, cut] + step_size * mass[at, :, cut] * moment

    rims(q, halo, nu, obs, nu_halo, obs_halo, scaled, deep, rim_scaled, scaled_deep, use)
    send_rims(rim_q, to_a, to_b)
    join(new_q, inner_q, rim_q)


def last_inner_kernel(q, nu, obs, p, mass, scaled, new_p, energy, deep, scaled_deep):
    chains, planes = q.shape[:2]
    totals = [0.0] * chains

    def use(chain, x, cut, slope):
        moment = p[chain, x - WIDE, :, cut] - (0.5 * step_size) * slope
        new_p[chain, x - WIDE, :, cut] = moment
        totals[chain] = totals[chain] + (0.5 * mass[x - WIDE, :, cut]) * (moment * moment)

    misfits = interior(q, nu, obs, scaled, deep, scaled_deep, use)
    for chain in range(chains):
        squares = 0.0
        for x in range(planes):
            for cut in tiles(q.shape[-1]):
                v = q[chain, x, :, cut]
                squares = squares + v * v
        energy[chain] = fold(
            (0.5 * inv_noise) * misfits[chain] + (0.5 * prior_weight) * squares + totals[chain]
        )


def last_rim_kernel(
    q, from_a, from_b, nu, obs, nu_halo, obs_halo, p, mass, scaled, inner_p, energy,
    potential, kinetic, new_p, rows, halo, deep, rim_scaled, scaled_deep, rim_p,
):
    chains, planes = q.shape[:2]
    totals = [0.0] * chains
    place_halo(halo, from_a, from_b)

    def use(chain, x, cut, slope):
        at = x if x < WIDE else x - planes + 2 * WIDE
        moment = p[chain, at, :, cut] - (0.5 * step_size) * slope
        rim_p[chain, at, :, cut] = moment
        totals[chain] = totals[chain] + (0.5 * mass[at, :, cut]) * (moment * moment)

    misfits = rims(
        q, halo, nu, obs, nu_halo, obs_halo, scaled, deep, rim_scaled, scaled_deep, use
    )
    join(new_p, inner_p, rim_p)
    sub = lax.broadcasted_iota(jnp.int32, (8, LANES), 0)
    lane = lax.broadcasted_iota(jnp.int32, (8, LANES), 1)
    mark = jnp.zeros((8, LANES), jnp.float32)
    for chain in range(chains):
        end = energy[chain] + fold((0.5 * inv_noise) * misfits[chain] + totals[chain])
        start = potential[chain] + kinetic[chain]
        for row, tile in enumerate((start, end)):
            mark = jnp.where((sub == row) & (lane == chain), jnp.sum(tile), mark)
    for i in range(rows.shape[0]):
        rows[i] = mark


def local(position, momentum_draw, viscosity, observed):
    chains, planes, depth, across = position.shape
    groups, slabs = lax.axis_size("chain"), lax.axis_size("gx")
    cells = planes * slabs * depth * across
    near = [(i, i ^ 1) for i in range(groups)]
    far = [(i, i ^ 2) for i in range(groups)]
    pair_a = [(i, i ^ 1) for i in range(slabs)]
    pair_b = [(i, (i + 1 if i % 2 else i - 1) % slabs) for i in range(slabs)]
    half = planes // 2
    plane = (depth, across)
    rest = planes - 2 * WIDE
    block = (chains, planes, *plane)
    rim_block = (chains, 2 * WIDE, *plane)
    inner_block = (chains, rest, *plane)
    halo = (2, chains, WIDE, *plane)
    edge = (chains * WIDE, *plane)
    sides = (2, *plane)
    tile = (chains, 8, LANES)
    scaled_shape = (chains, planes - 2, *plane)
    field = (chains, planes + 2 * WIDE, *plane)
    inner_scratch = [block, scaled_shape]
    rim_scratch = [halo, field, rim_block, (chains, planes + 2, *plane)]
    work = chains * planes * depth * across * 30

    def swap(to_a, to_b):
        return lax.ppermute(to_a, "gx", pair_a), lax.ppermute(to_b, "gx", pair_b)

    memory = pl.BlockSpec(memory_space=pl.ANY)
    first_edge = (chains * WIDE + 2, *plane)
    to_a, to_b = call(
        fetch_kernel, [first_edge, first_edge], [pltpu.SemaphoreType.DMA((2 * (chains + 2),))],
        "fetch", work // 16, [memory] * 3,
    )(position, viscosity, observed)
    from_a, from_b = swap(to_a, to_b)
    sums = (half, 2, *plane)
    keep, send = call(sums_kernel, [sums, sums], [], "sums", work // 16)(position)
    got = lax.ppermute(send, "chain", near)
    part, inner_part = call(
        add_kernel, [(WIDE, 2, *plane), (half - WIDE, 2, *plane)], [], "add", work // 16
    )(keep, got)
    far_part = lax.ppermute(part, "chain", far)
    far_inner = lax.ppermute(inner_part, "chain", far)
    scaled, inner_slope, potential = call(
        first_inner_kernel, [scaled_shape, inner_block, tile], inner_scratch, "first_inner", work
    )(position, viscosity, observed)
    slope, nu_halo, obs_halo, potential = call(
        first_rim_kernel, [rim_block, sides, sides, tile], rim_scratch, "first_rim", work
    )(position, from_a, from_b, viscosity, observed, scaled, potential)

    def mass_body(*refs):
        mass_kernel(chains * groups, *refs)

    def mass_of(own, remote, name):
        shape = (own.shape[0], *plane)
        mine = call(mass_body, [shape], [], name, work // 16)(own, remote)[0]
        return mine, lax.ppermute(mine, "chain", near)

    mine, other = mass_of(part, far_part, "mass_rim")
    rim_q, rim_p, rim_mass, kinetic, to_a, to_b = call(
        launch_rim_kernel,
        [rim_block, rim_block, (2 * WIDE, *plane), tile, edge, edge],
        [], "launch_rim", work // 4,
    )(position, momentum_draw, slope, mine, other)
    from_a, from_b = swap(to_a, to_b)
    mine, other = mass_of(inner_part, far_inner, "mass_inner")
    q, inner_p, inner_mass, kinetic = call(
        launch_inner_kernel,
        [block, inner_block, (rest, *plane), tile],
        [inner_block, inner_block], "launch_inner", work // 4,
    )(position, momentum_draw, inner_slope, mine, other, rim_q, kinetic)
    for _ in range(LEAPS - 1):
        scaled, inner_q, inner_p = call(
            leap_inner_kernel, [scaled_shape, inner_block, inner_block], inner_scratch, "leap_inner", work
        )(q, viscosity, observed, inner_p, inner_mass)
        q, rim_p, to_a, to_b = call(
            leap_rim_kernel, [block, rim_block, edge, edge], [*rim_scratch, rim_block], "leap_rim", work
        )(q, from_a, from_b, viscosity, observed, nu_halo, obs_halo, rim_p, rim_mass, scaled, inner_q)
        from_a, from_b = swap(to_a, to_b)
    scaled, inner_p, energy = call(
        last_inner_kernel, [scaled_shape, inner_block, tile], inner_scratch, "last_inner", work
    )(q, viscosity, observed, inner_p, inner_mass)
    p, rows = call(
        last_rim_kernel, [block, (slabs, 8, LANES)], [*rim_scratch, rim_block], "last_rim", work
    )(
        q, from_a, from_b, viscosity, observed, nu_halo, obs_halo, rim_p, rim_mass,
        scaled, inner_p, energy, potential, kinetic,
    )
    rows = lax.all_to_all(rows, "gx", 0, 0, tiled=True)
    energies = jnp.sum(rows[:, :2, :chains], axis=0) / cells
    return (q, p, energies)


def solution(mesh):
    in_specs = (
        P("chain", "gx", None, None),
        P("chain", "gx", None, None),
        P("gx", None, None),
        P("gx", None, None),
    )
    out_specs = (P("chain", "gx", None, None), P("chain", "gx", None, None), P(None, "chain"))
    return jax.shard_map(local, mesh=mesh, in_specs=in_specs, out_specs=out_specs, check_vma=False)
```

```python
import jax
import jax.numpy as jnp
from jax import lax
from jax.experimental import pallas as pl
from jax.experimental.pallas import tpu as pltpu
from jax.sharding import PartitionSpec as P

LEAPS = 2

unit = -0.05
inv_noise = 0.25
prior_weight = 0.5
step_size = 0.05
LANES = 128
WIDE = 2


VECTOR = pl.BlockSpec(memory_space=pltpu.VMEM)
MEMORY = pl.BlockSpec(memory_space=pltpu.HBM)


def call(kernel, out_shapes, scratch, name, work, ins=None, outs=None, aliases=None, limit=32):
    more = {} if ins is None else {"in_specs": ins}
    if aliases:
        more["input_output_aliases"] = aliases
    return pl.pallas_call(
        kernel,
        out_shape=[jax.ShapeDtypeStruct(shape, jnp.float32) for shape in out_shapes],
        out_specs=outs or [VECTOR] * len(out_shapes),
        scratch_shapes=[
            pltpu.VMEM(shape, jnp.float32) if isinstance(shape, tuple) else shape
            for shape in scratch
        ],
        compiler_params=pltpu.CompilerParams(vmem_limit_bytes=limit << 20),
        cost_estimate=pl.CostEstimate(flops=work, bytes_accessed=work // 8, transcendentals=0),
        name=name,
        **more,
    )


def tiles(width):
    return [slice(j * LANES, (j + 1) * LANES) for j in range(width // LANES)]


def depth_sum(v):
    depth = v.shape[0]
    row = lax.broadcasted_iota(jnp.int32, v.shape, 0)
    below = jnp.where(row == 0, 0.0, pltpu.roll(v, 1, 0))
    above = jnp.where(row == depth - 1, 0.0, pltpu.roll(v, depth - 1, 0))
    return below + above


def stencil(planes, deeps):
    cuts = tiles(planes[1].shape[-1])
    edge_terms, own_terms = [], []
    for cut in cuts:
        v = planes[1][:, cut]
        w = deeps[1][:, cut] + (planes[0][:, cut] + planes[2][:, cut])
        corner = deeps[0][:, cut] + deeps[2][:, cut]
        t = 6.0 * v + (2.0 * w + corner)
        d = t + w
        edge_terms.append(t)
        own_terms.append((d + d) - 92.0 * v)
    lane = lax.broadcasted_iota(jnp.int32, edge_terms[0].shape, 1)
    ups = [pltpu.roll(t, 1, 1) for t in edge_terms]
    downs = [pltpu.roll(t, LANES - 1, 1) for t in edge_terms]
    result = []
    for j in range(len(cuts)):
        before = ups[j - 1] if j else 0.0
        after = downs[j + 1] if j + 1 < len(cuts) else 0.0
        left = jnp.where(lane == 0, before, ups[j])
        right = jnp.where(lane == LANES - 1, after, downs[j])
        result.append(own_terms[j] + (left + right))
    return list(zip(cuts, result, strict=True))


def deepen(deep, source):
    for cut in tiles(source.shape[-1]):
        deep[:, cut] = depth_sum(source[:, cut])


def weigh(view, deep, nu, target, out, out_deep):
    total = 0.0
    for cut, k in stencil(view, deep):
        n = nu[:, cut]
        misfit = (unit * n) * k - target[:, cut]
        s = n * misfit
        out[:, cut] = s
        out_deep[:, cut] = depth_sum(s)
        total = total + misfit * misfit
    return total


def fold(total):
    return total[:8] + total[8:]


def whole(q):
    return lambda chain, x: q.at[chain, x]


def parts(rim, inner):
    planes = inner.shape[1] + 2 * WIDE

    def at(chain, x):
        if x < WIDE:
            return rim.at[chain, x]
        if x >= planes - WIDE:
            return rim.at[chain, x - planes + 2 * WIDE]
        return inner.at[chain, x - WIDE]

    return at


def interior(q_at, nu, obs, scaled, deep, scaled_deep, use):
    chains, planes = deep.shape[:2]
    totals = []
    for chain in range(chains):
        for x in range(planes):
            deepen(deep.at[chain, x], q_at(chain, x))
    for chain in range(chains):
        total = 0.0
        for x in range(1, planes - 1):
            near = range(x - 1, x + 2)
            total = total + weigh(
                [q_at(chain, i) for i in near],
                [deep.at[chain, i] for i in near],
                nu.at[x],
                obs.at[x],
                scaled.at[chain, x - 1],
                scaled_deep.at[chain, x - 1],
            )
        totals.append(total)
    for chain in range(chains):
        for x in range(2, planes - 2):
            near = range(x - 2, x + 1)
            view = [scaled.at[chain, i] for i in near]
            for cut, k in stencil(view, [scaled_deep.at[chain, i] for i in near]):
                v = q_at(chain, x)[:, cut]
                use(chain, x, cut, v, (inv_noise * unit) * k + prior_weight * v)
    return totals


def parity():
    return lax.rem(lax.axis_index("gx"), 2)


def place_halo(halo, from_a, from_b):
    odd = parity()
    chains = halo.shape[1]
    for chain in range(chains):
        for i in range(WIDE):
            halo[1 - odd, chain, i] = from_a[chain * WIDE + i]
            halo[odd, chain, i] = from_b[chain * WIDE + i]


def rims(q_at, halo, nu, obs, nu_halo, obs_halo, scaled, deep, rim_scaled, scaled_deep, use):
    chains, planes = scaled.shape[0], scaled.shape[1] + 2

    def at(chain, x):
        if x < 0:
            return halo.at[0, chain, WIDE + x]
        if x >= planes:
            return halo.at[1, chain, x - planes]
        return q_at(chain, x)

    def scaled_at(chain, x):
        if x in (-1, 0):
            return rim_scaled.at[chain, x + 1]
        if x in (planes - 1, planes):
            return rim_scaled.at[chain, x - planes + 3]
        return scaled.at[chain, x - 1]

    sides = ((-2, -1, 0, 1), (planes + 1, planes, planes - 1, planes - 2))
    totals = []
    for chain in range(chains):
        for side in sides:
            for x in side:
                deepen(deep.at[chain, x + WIDE], at(chain, x))
    for chain in range(chains):
        total = 0.0
        for s, side in enumerate(sides):
            for x in side[1:3]:
                outer = x == side[1]
                near = range(x - 1, x + 2)
                squares = weigh(
                    [at(chain, i) for i in near],
                    [deep.at[chain, i + WIDE] for i in near],
                    nu_halo.at[s] if outer else nu.at[x],
                    obs_halo.at[s] if outer else obs.at[x],
                    scaled_at(chain, x),
                    scaled_deep.at[chain, x + 1],
                )
                total = total if outer else total + squares
            for x in (1, 2) if s == 0 else (planes - 2, planes - 3):
                deepen(scaled_deep.at[chain, x + 1], scaled_at(chain, x))
        totals.append(total)
    for chain in range(chains):
        for x in (0, 1, planes - 2, planes - 1):
            near = range(x - 1, x + 2)
            view = [scaled_at(chain, i) for i in near]
            for cut, k in stencil(view, [scaled_deep.at[chain, i + 1] for i in near]):
                v = q_at(chain, x)[:, cut]
                use(chain, x, cut, v, (inv_noise * unit) * k + prior_weight * v)
    return totals


def entry_kernel(q, nu, obs, own, keep, send, to_a, to_b, sems):
    core, odd = lax.rem(lax.axis_index("chain"), 2), parity()
    chains, planes = own.shape[:2]
    half = planes // 2
    load = [pltpu.make_async_copy(q.at[chain], own.at[chain], sems.at[chain]) for chain in range(chains)]
    edges = []
    for i, (source, at) in enumerate(((nu, chains * WIDE), (obs, chains * WIDE + 1))):
        for k, (out, low) in enumerate(((to_a, odd), (to_b, 1 - odd))):
            edges.append(
                pltpu.make_async_copy(
                    source.at[(1 - low) * (planes - 1)], out.at[at], sems.at[chains + 2 * i + k]
                )
            )
    for copy in load + edges:
        copy.start()
    for copy in load:
        copy.wait()
    for chain in range(chains):
        for i in range(WIDE):
            to_a[chain * WIDE + i] = own[chain, (1 - odd) * (planes - WIDE) + i]
            to_b[chain * WIDE + i] = own[chain, odd * (planes - WIDE) + i]
    for x in range(half):
        for out, base in ((keep, core * half), (send, (1 - core) * half)):
            for cut in tiles(own.shape[-1]):
                first = own[0, base + x, :, cut]
                second = first * first
                for chain in range(1, chains):
                    v = own[chain, base + x, :, cut]
                    first = first + v
                    second = second + v * v
                out[x, 0, :, cut] = first
                out[x, 1, :, cut] = second
    for copy in edges:
        copy.wait()


def add_kernel(rim, a, b, *rest):
    core = lax.rem(lax.axis_index("chain"), 2)
    out = rest[-1]
    count = out.shape[0]
    for x in range(count):
        at = (core if rim else 1 - core) * count + x
        out[x] = a[at] + b[at]


def mass_kernel(count, a, b, *rest):
    out = rest[-1]
    for x in range(a.shape[0]):
        mean = (a[x, 0] + b[x, 0]) / count
        out[x] = 0.5 + (a[x, 1] + b[x, 1]) / count - mean * mean


def first_inner_kernel(q, nu, obs, scaled, slope, potential, deep, scaled_deep):
    chains, planes = q.shape[:2]

    def use(chain, x, cut, v, value):
        slope[chain, x - 2, :, cut] = value

    misfits = interior(whole(q), nu, obs, scaled, deep, scaled_deep, use)
    for chain in range(chains):
        squares = 0.0
        for x in range(planes):
            for cut in tiles(q.shape[-1]):
                v = q[chain, x, :, cut]
                squares = squares + v * v
        potential[chain] = fold(
            (0.5 * inv_noise) * misfits[chain] + (0.5 * prior_weight) * squares
        )


def first_rim_kernel(
    q, from_a, from_b, nu, obs, scaled, before,
    slope, nu_halo, obs_halo, potential, halo, deep, rim_scaled, scaled_deep,
):
    odd = parity()
    chains, planes = q.shape[:2]
    place_halo(halo, from_a, from_b)
    for out, at in ((nu_halo, chains * WIDE), (obs_halo, chains * WIDE + 1)):
        out[1 - odd] = from_a[at]
        out[odd] = from_b[at]

    def use(chain, x, cut, v, value):
        slope[chain, x if x < 2 else x - planes + 4, :, cut] = value

    misfits = rims(
        whole(q), halo, nu, obs, nu_halo, obs_halo, scaled, deep, rim_scaled, scaled_deep, use
    )
    for chain in range(chains):
        potential[chain] = before[chain] + fold((0.5 * inv_noise) * misfits[chain])


def launch(q, draw, slope, mine, other, base, new_q, new_p, mass, totals):
    chains = q.shape[0]
    for part, (start, offset) in ((mine, base[0]), (other, base[1])):
        for i in range(part.shape[0]):
            for cut in tiles(q.shape[-1]):
                im = part[i, :, cut]
                mass[offset + i, :, cut] = im
                inverse_root = 1.0 / jnp.sqrt(im)
                for chain in range(chains):
                    p = draw[chain, start + i, :, cut] * inverse_root
                    totals[chain] = totals[chain] + im * p * p
                    p = p - (0.5 * step_size) * slope[chain, offset + i, :, cut]
                    new_p[chain, offset + i, :, cut] = p
                    new_q[chain, offset + i, :, cut] = (
                        q[chain, start + i, :, cut] + step_size * im * p
                    )


def send_rims(source, to_a, to_b):
    odd = parity()
    for chain in range(source.shape[0]):
        for i in range(WIDE):
            to_a[chain * WIDE + i] = source[chain, (1 - odd) * WIDE + i]
            to_b[chain * WIDE + i] = source[chain, odd * WIDE + i]


def launch_rim_kernel(q, draw, slope, mine, other, new_q, new_p, mass, kinetic, to_a, to_b):
    core = lax.rem(lax.axis_index("chain"), 2)
    chains, planes = q.shape[:2]
    far = planes - WIDE
    totals = [0.0] * chains
    base = ((core * far, core * WIDE), ((1 - core) * far, (1 - core) * WIDE))
    launch(q, draw, slope, mine, other, base, new_q, new_p, mass, totals)
    for chain in range(chains):
        kinetic[chain] = fold(0.5 * totals[chain])
    send_rims(new_q, to_a, to_b)


def launch_inner_kernel(q, draw, slope, mine, other, before, new_q, new_p, mass, kinetic):
    core = lax.rem(lax.axis_index("chain"), 2)
    chains, planes = q.shape[:2]
    half = planes // 2 - WIDE
    totals = [0.0] * chains
    base = tuple((WIDE + c * half, c * half) for c in (core, 1 - core))
    launch(q, draw, slope, mine, other, base, new_q, new_p, mass, totals)
    for chain in range(chains):
        kinetic[chain] = before[chain] + fold(0.5 * totals[chain])


def leap_inner_kernel(q_rim, q_inner, nu, obs, p, mass, scaled, new_q, new_p, deep, scaled_deep):
    def use(chain, x, cut, v, slope):
        at = x - WIDE
        moment = p[chain, at, :, cut] - step_size * slope
        new_p[chain, at, :, cut] = moment
        new_q[chain, at, :, cut] = v + step_size * mass[at, :, cut] * moment

    interior(parts(q_rim, q_inner), nu, obs, scaled, deep, scaled_deep, use)


def rim_index(x, planes):
    return x if x < WIDE else x - planes + 2 * WIDE


def leap_rim_kernel(
    q_rim, q_inner, from_a, from_b, nu, obs, nu_halo, obs_halo, p, mass, scaled,
    new_q, new_p, to_a, to_b, halo, deep, rim_scaled, scaled_deep,
):
    planes = q_inner.shape[1] + 2 * WIDE
    place_halo(halo, from_a, from_b)

    def use(chain, x, cut, v, slope):
        at = rim_index(x, planes)
        moment = p[chain, at, :, cut] - step_size * slope
        new_p[chain, at, :, cut] = moment
        new_q[chain, at, :, cut] = v + step_size * mass[at, :, cut] * moment

    rims(
        parts(q_rim, q_inner), halo, nu, obs, nu_halo, obs_halo,
        scaled, deep, rim_scaled, scaled_deep, use,
    )
    send_rims(new_q, to_a, to_b)


def run(copies):
    for copy in copies:
        copy.start()
    for copy in copies:
        copy.wait()


def rim_copies(rim, out, sems):
    chains, planes = out.shape[:2]
    copies = []
    for chain in range(chains):
        for side, start in enumerate((0, planes - WIDE)):
            copies.append(
                pltpu.make_async_copy(
                    rim.at[chain, pl.ds(side * WIDE, WIDE)],
                    out.at[chain, pl.ds(start, WIDE)],
                    sems.at[2 * chain + side],
                )
            )
    return copies


def inner_copies(inner, out, sems):
    chains, planes = out.shape[:2]
    return [
        pltpu.make_async_copy(
            inner.at[chain], out.at[chain, pl.ds(WIDE, planes - 2 * WIDE)], sems.at[2 * chains + chain]
        )
        for chain in range(chains)
    ]


def store_kernel(rim, inner, out, token, sems):
    token[...] = jnp.zeros_like(token)
    run(rim_copies(rim, out, sems) + inner_copies(inner, out, sems))


def store_inner_kernel(inner, out, sems):
    run(inner_copies(inner, out, sems))


def last_inner_kernel(q_rim, q_inner, nu, obs, p, mass, scaled, new_p, energy, deep, scaled_deep):
    chains, planes = deep.shape[:2]
    q_at = parts(q_rim, q_inner)
    totals = [0.0] * chains

    def use(chain, x, cut, v, slope):
        at = x - WIDE
        moment = p[chain, at, :, cut] - (0.5 * step_size) * slope
        new_p[chain, at, :, cut] = moment
        totals[chain] = totals[chain] + (0.5 * mass[at, :, cut]) * (moment * moment)

    misfits = interior(q_at, nu, obs, scaled, deep, scaled_deep, use)
    for chain in range(chains):
        squares = 0.0
        for x in range(planes):
            view = q_at(chain, x)
            for cut in tiles(view.shape[-1]):
                v = view[:, cut]
                squares = squares + v * v
        energy[chain] = fold(
            (0.5 * inv_noise) * misfits[chain] + (0.5 * prior_weight) * squares + totals[chain]
        )


def last_rim_kernel(
    q_rim, q_inner, from_a, from_b, nu, obs, nu_halo, obs_halo, p, mass, scaled, energy,
    potential, kinetic, stored, partial_p,
    new_p, rows, halo, deep, rim_scaled, scaled_deep, rim_p, sems,
):
    chains, planes = new_p.shape[:2]
    totals = [0.0] * chains
    place_halo(halo, from_a, from_b)

    def use(chain, x, cut, v, slope):
        at = rim_index(x, planes)
        moment = p[chain, at, :, cut] - (0.5 * step_size) * slope
        rim_p[chain, at, :, cut] = moment
        totals[chain] = totals[chain] + (0.5 * mass[at, :, cut]) * (moment * moment)

    misfits = rims(
        parts(q_rim, q_inner), halo, nu, obs, nu_halo, obs_halo,
        scaled, deep, rim_scaled, scaled_deep, use,
    )
    copies = rim_copies(rim_p, new_p, sems)
    for copy in copies:
        copy.start()
    sub = lax.broadcasted_iota(jnp.int32, (8, LANES), 0)
    lane = lax.broadcasted_iota(jnp.int32, (8, LANES), 1)
    mark = jnp.zeros((8, LANES), jnp.float32)
    for chain in range(chains):
        end = energy[chain] + fold((0.5 * inv_noise) * misfits[chain] + totals[chain])
        start = potential[chain] + kinetic[chain]
        for row, tile in enumerate((start, end)):
            mark = jnp.where((sub == row) & (lane == chain), jnp.sum(tile), mark)
    for i in range(rows.shape[0]):
        rows[i] = mark
    for copy in copies:
        copy.wait()


def local(position, momentum_draw, viscosity, observed):
    chains, planes, depth, across = position.shape
    groups, slabs = lax.axis_size("chain"), lax.axis_size("gx")
    cells = planes * slabs * depth * across
    near = [(i, i ^ 1) for i in range(groups)]
    far = [(i, i ^ 2) for i in range(groups)]
    pair_a = [(i, i ^ 1) for i in range(slabs)]
    pair_b = [(i, (i + 1 if i % 2 else i - 1) % slabs) for i in range(slabs)]
    half = planes // 2
    plane = (depth, across)
    rest = planes - 2 * WIDE
    block = (chains, planes, *plane)
    rim_block = (chains, 2 * WIDE, *plane)
    inner_block = (chains, rest, *plane)
    halo = (2, chains, WIDE, *plane)
    edge = (chains * WIDE, *plane)
    sides = (2, *plane)
    tile = (chains, 8, LANES)
    scaled_shape = (chains, planes - 2, *plane)
    field = (chains, planes + 2 * WIDE, *plane)
    inner_scratch = [block, scaled_shape]
    rim_scratch = [halo, field, rim_block, (chains, planes + 2, *plane)]
    work = chains * planes * depth * across * 30

    def swap(to_a, to_b):
        return lax.ppermute(to_a, "gx", pair_a), lax.ppermute(to_b, "gx", pair_b)

    first_edge = (chains * WIDE + 2, *plane)
    sums = (half, 2, *plane)
    position, keep, send, to_a, to_b = call(
        entry_kernel, [block, sums, sums, first_edge, first_edge],
        [pltpu.SemaphoreType.DMA((chains + 4,))], "entry", work // 16, [MEMORY] * 3,
    )(*(pltpu.with_memory_space_constraint(a, pltpu.HBM) for a in (position, viscosity, observed)))
    from_a, from_b = swap(to_a, to_b)
    got = lax.ppermute(send, "chain", near)

    def mass_body(*refs):
        mass_kernel(chains * groups, *refs)

    def mass_of(count, rim, after, before_mass, name):
        def add_body(*refs):
            add_kernel(rim, *refs)

        part = call(add_body, [(count, 2, *plane)], [], name + "_add", work // 16)(keep, got, *after)[0]
        remote = lax.ppermute(part, "chain", far)
        mine = call(mass_body, [(count, *plane)], [], name, work // 16)(part, remote, *before_mass)[0]
        return mine, lax.ppermute(mine, "chain", near)

    scaled, inner_slope, potential = call(
        first_inner_kernel, [scaled_shape, inner_block, tile], inner_scratch, "first_inner", work
    )(position, viscosity, observed)
    mine, other = mass_of(WIDE, True, (), (potential,), "mass_rim")
    inner_mine, inner_other = mass_of(half - WIDE, False, (mine,), (), "mass_inner")
    slope, nu_halo, obs_halo, potential = call(
        first_rim_kernel, [rim_block, sides, sides, tile], rim_scratch, "first_rim", work
    )(position, from_a, from_b, viscosity, observed, scaled, potential)
    rim_q, rim_p, rim_mass, kinetic, to_a, to_b = call(
        launch_rim_kernel,
        [rim_block, rim_block, (2 * WIDE, *plane), tile, edge, edge],
        [], "launch_rim", work // 4,
    )(position, momentum_draw, slope, mine, other)
    from_a, from_b = swap(to_a, to_b)
    inner_q, inner_p, inner_mass, kinetic = call(
        launch_inner_kernel,
        [inner_block, inner_block, (rest, *plane), tile],
        [], "launch_inner", work // 4,
    )(position, momentum_draw, inner_slope, inner_mine, inner_other, kinetic)
    for _ in range(LEAPS - 1):
        old_rim, old_inner = rim_q, inner_q
        scaled, inner_q, inner_p = call(
            leap_inner_kernel, [scaled_shape, inner_block, inner_block], inner_scratch, "leap_inner", work
        )(old_rim, old_inner, viscosity, observed, inner_p, inner_mass)
        rim_q, rim_p, to_a, to_b = call(
            leap_rim_kernel, [rim_block, rim_block, edge, edge], rim_scratch, "leap_rim", work
        )(
            old_rim, old_inner, from_a, from_b, viscosity, observed, nu_halo, obs_halo,
            rim_p, rim_mass, scaled,
        )
        from_a, from_b = swap(to_a, to_b)
    copy_sems = pltpu.SemaphoreType.DMA((3 * chains,))
    q, stored = call(
        store_kernel, [block, (8, LANES)], [copy_sems], "store_q", work // 8, outs=[MEMORY, VECTOR]
    )(rim_q, inner_q)
    scaled, inner_p, energy = call(
        last_inner_kernel, [scaled_shape, inner_block, tile], inner_scratch, "last_inner", work
    )(rim_q, inner_q, viscosity, observed, inner_p, inner_mass)
    partial_p = call(
        store_inner_kernel, [block], [copy_sems], "store_p", work // 16, outs=[MEMORY]
    )(inner_p)[0]
    operands = (
        rim_q, inner_q, from_a, from_b, viscosity, observed, nu_halo, obs_halo, rim_p, rim_mass,
        scaled, energy, potential, kinetic, stored, partial_p,
    )
    p, rows = call(
        last_rim_kernel, [block, (slabs, 8, LANES)], [*rim_scratch, rim_block, copy_sems], "last_rim", work,
        [VECTOR] * (len(operands) - 1) + [MEMORY], [MEMORY, VECTOR], {len(operands) - 1: 0},
    )(*operands)
    rows = lax.all_to_all(rows, "gx", 0, 0, tiled=True)
    energies = jnp.sum(rows[:, :2, :chains], axis=0) / cells
    return (q, p, energies)


def solution(mesh):
    in_specs = (
        P("chain", "gx", None, None),
        P("chain", "gx", None, None),
        P("gx", None, None),
        P("gx", None, None),
    )
    out_specs = (P("chain", "gx", None, None), P("chain", "gx", None, None), P(None, "chain"))
    return jax.shard_map(local, mesh=mesh, in_specs=in_specs, out_specs=out_specs, check_vma=False)
```

```python
import jax
import jax.numpy as jnp
from jax import lax
from jax.experimental import pallas as pl
from jax.experimental.pallas import tpu as pltpu
from jax.sharding import PartitionSpec as P

LEAPS = 2

unit = -0.05
inv_noise = 0.25
prior_weight = 0.5
step_size = 0.05
LANES = 128
WIDE = 2


VECTOR = pl.BlockSpec(memory_space=pltpu.VMEM)
MEMORY = pl.BlockSpec(memory_space=pltpu.HBM)


def call(kernel, out_shapes, scratch, name, work, ins=None, outs=None, aliases=None, limit=32):
    more = {} if ins is None else {"in_specs": ins}
    if aliases:
        more["input_output_aliases"] = aliases
    return pl.pallas_call(
        kernel,
        out_shape=[jax.ShapeDtypeStruct(shape, jnp.float32) for shape in out_shapes],
        out_specs=outs or [VECTOR] * len(out_shapes),
        scratch_shapes=[
            pltpu.VMEM(shape, jnp.float32) if isinstance(shape, tuple) else shape
            for shape in scratch
        ],
        compiler_params=pltpu.CompilerParams(vmem_limit_bytes=limit << 20),
        cost_estimate=pl.CostEstimate(flops=work, bytes_accessed=work // 8, transcendentals=0),
        name=name,
        **more,
    )


def tiles(width):
    return [slice(j * LANES, (j + 1) * LANES) for j in range(width // LANES)]


def depth_sum(v):
    depth = v.shape[0]
    row = lax.broadcasted_iota(jnp.int32, v.shape, 0)
    below = jnp.where(row == 0, 0.0, pltpu.roll(v, 1, 0))
    above = jnp.where(row == depth - 1, 0.0, pltpu.roll(v, depth - 1, 0))
    return below + above


def stencil(planes, deeps):
    cuts = tiles(planes[1].shape[-1])
    edge_terms, own_terms = [], []
    for cut in cuts:
        v = planes[1][:, cut]
        w = deeps[1][:, cut] + (planes[0][:, cut] + planes[2][:, cut])
        corner = deeps[0][:, cut] + deeps[2][:, cut]
        t = 6.0 * v + (2.0 * w + corner)
        d = t + w
        edge_terms.append(t)
        own_terms.append((d + d) - 92.0 * v)
    lane = lax.broadcasted_iota(jnp.int32, edge_terms[0].shape, 1)
    ups = [pltpu.roll(t, 1, 1) for t in edge_terms]
    downs = [pltpu.roll(t, LANES - 1, 1) for t in edge_terms]
    result = []
    for j in range(len(cuts)):
        before = ups[j - 1] if j else 0.0
        after = downs[j + 1] if j + 1 < len(cuts) else 0.0
        left = jnp.where(lane == 0, before, ups[j])
        right = jnp.where(lane == LANES - 1, after, downs[j])
        result.append(own_terms[j] + (left + right))
    return list(zip(cuts, result, strict=True))


def deepen(deep, source):
    for cut in tiles(source.shape[-1]):
        deep[:, cut] = depth_sum(source[:, cut])


def weigh(view, deep, nu, target, out, out_deep):
    total = 0.0
    for cut, k in stencil(view, deep):
        n = nu[:, cut]
        misfit = (unit * n) * k - target[:, cut]
        s = n * misfit
        out[:, cut] = s
        out_deep[:, cut] = depth_sum(s)
        total = total + misfit * misfit
    return total


def fold(total):
    return total[:8] + total[8:]


def whole(q):
    return lambda chain, x: q.at[chain, x]


def parts(rim, inner):
    planes = inner.shape[1] + 2 * WIDE

    def at(chain, x):
        if x < WIDE:
            return rim.at[chain, x]
        if x >= planes - WIDE:
            return rim.at[chain, x - planes + 2 * WIDE]
        return inner.at[chain, x - WIDE]

    return at


def interior(q_at, nu, obs, scaled, deep, scaled_deep, use):
    chains, planes = deep.shape[:2]
    totals = []
    for chain in range(chains):
        for x in range(planes):
            deepen(deep.at[chain, x], q_at(chain, x))
    for chain in range(chains):
        total = 0.0
        for x in range(1, planes - 1):
            near = range(x - 1, x + 2)
            total = total + weigh(
                [q_at(chain, i) for i in near],
                [deep.at[chain, i] for i in near],
                nu.at[x],
                obs.at[x],
                scaled.at[chain, x - 1],
                scaled_deep.at[chain, x - 1],
            )
        totals.append(total)
    for chain in range(chains):
        for x in range(2, planes - 2):
            near = range(x - 2, x + 1)
            view = [scaled.at[chain, i] for i in near]
            for cut, k in stencil(view, [scaled_deep.at[chain, i] for i in near]):
                v = q_at(chain, x)[:, cut]
                use(chain, x, cut, v, (inv_noise * unit) * k + prior_weight * v)
    return totals


def parity():
    return lax.rem(lax.axis_index("gx"), 2)


def place_halo(halo, from_a, from_b):
    odd = parity()
    chains = halo.shape[1]
    for chain in range(chains):
        for i in range(WIDE):
            halo[1 - odd, chain, i] = from_a[chain * WIDE + i]
            halo[odd, chain, i] = from_b[chain * WIDE + i]


def rims(
    q_at, halo, nu, obs, nu_halo, obs_halo, scaled, deep, rim_scaled, scaled_deep, use, ready=None
):
    chains, planes = scaled.shape[0], scaled.shape[1] + 2

    def at(chain, x):
        if x < 0:
            return halo.at[0, chain, WIDE + x]
        if x >= planes:
            return halo.at[1, chain, x - planes]
        return q_at(chain, x)

    def scaled_at(chain, x):
        if x in (-1, 0):
            return rim_scaled.at[chain, x + 1]
        if x in (planes - 1, planes):
            return rim_scaled.at[chain, x - planes + 3]
        return scaled.at[chain, x - 1]

    sides = ((-2, -1, 0, 1), (planes + 1, planes, planes - 1, planes - 2))
    totals = []
    for chain in range(chains):
        for side in sides:
            for x in side:
                deepen(deep.at[chain, x + WIDE], at(chain, x))
    for chain in range(chains):
        total = 0.0
        for s, side in enumerate(sides):
            for x in side[1:3]:
                outer = x == side[1]
                near = range(x - 1, x + 2)
                squares = weigh(
                    [at(chain, i) for i in near],
                    [deep.at[chain, i + WIDE] for i in near],
                    nu_halo.at[s] if outer else nu.at[x],
                    obs_halo.at[s] if outer else obs.at[x],
                    scaled_at(chain, x),
                    scaled_deep.at[chain, x + 1],
                )
                total = total if outer else total + squares
            for x in (1, 2) if s == 0 else (planes - 2, planes - 3):
                deepen(scaled_deep.at[chain, x + 1], scaled_at(chain, x))
        totals.append(total)
    for chain in range(chains):
        for x in (0, 1, planes - 2, planes - 1):
            near = range(x - 1, x + 2)
            view = [scaled_at(chain, i) for i in near]
            for cut, k in stencil(view, [scaled_deep.at[chain, i + 1] for i in near]):
                v = q_at(chain, x)[:, cut]
                use(chain, x, cut, v, (inv_noise * unit) * k + prior_weight * v)
            if ready and x in (1, planes - 1):
                ready(chain, x > 1)
    return totals


def entry_kernel(q, nu, obs, own, keep, send, to_a, to_b, sems):
    core, odd = lax.rem(lax.axis_index("chain"), 2), parity()
    chains, planes = own.shape[:2]
    half = planes // 2
    load = [pltpu.make_async_copy(q.at[chain], own.at[chain], sems.at[chain]) for chain in range(chains)]
    edges = []
    for i, (source, at) in enumerate(((nu, chains * WIDE), (obs, chains * WIDE + 1))):
        for k, (out, low) in enumerate(((to_a, odd), (to_b, 1 - odd))):
            edges.append(
                pltpu.make_async_copy(
                    source.at[(1 - low) * (planes - 1)], out.at[at], sems.at[chains + 2 * i + k]
                )
            )
    for copy in load + edges:
        copy.start()
    for copy in load:
        copy.wait()
    for chain in range(chains):
        for i in range(WIDE):
            to_a[chain * WIDE + i] = own[chain, (1 - odd) * (planes - WIDE) + i]
            to_b[chain * WIDE + i] = own[chain, odd * (planes - WIDE) + i]
    for x in range(half):
        for out, base in ((keep, core * half), (send, (1 - core) * half)):
            for cut in tiles(own.shape[-1]):
                first = own[0, base + x, :, cut]
                second = first * first
                for chain in range(1, chains):
                    v = own[chain, base + x, :, cut]
                    first = first + v
                    second = second + v * v
                out[x, 0, :, cut] = first
                out[x, 1, :, cut] = second
    for copy in edges:
        copy.wait()


def add_kernel(rim, a, b, *rest):
    core = lax.rem(lax.axis_index("chain"), 2)
    out = rest[-1]
    count = out.shape[0]
    for x in range(count):
        at = (core if rim else 1 - core) * count + x
        out[x] = a[at] + b[at]


def mass_kernel(count, a, b, *rest):
    out = rest[-1]
    for x in range(a.shape[0]):
        mean = (a[x, 0] + b[x, 0]) / count
        out[x] = 0.5 + (a[x, 1] + b[x, 1]) / count - mean * mean


def first_inner_kernel(q, nu, obs, scaled, slope, potential, deep, scaled_deep):
    chains, planes = q.shape[:2]

    def use(chain, x, cut, v, value):
        slope[chain, x - 2, :, cut] = value

    misfits = interior(whole(q), nu, obs, scaled, deep, scaled_deep, use)
    for chain in range(chains):
        squares = 0.0
        for x in range(planes):
            for cut in tiles(q.shape[-1]):
                v = q[chain, x, :, cut]
                squares = squares + v * v
        potential[chain] = fold(
            (0.5 * inv_noise) * misfits[chain] + (0.5 * prior_weight) * squares
        )


def first_rim_kernel(
    q, from_a, from_b, nu, obs, scaled, before,
    slope, nu_halo, obs_halo, potential, halo, deep, rim_scaled, scaled_deep,
):
    odd = parity()
    chains, planes = q.shape[:2]
    place_halo(halo, from_a, from_b)
    for out, at in ((nu_halo, chains * WIDE), (obs_halo, chains * WIDE + 1)):
        out[1 - odd] = from_a[at]
        out[odd] = from_b[at]

    def use(chain, x, cut, v, value):
        slope[chain, x if x < 2 else x - planes + 4, :, cut] = value

    misfits = rims(
        whole(q), halo, nu, obs, nu_halo, obs_halo, scaled, deep, rim_scaled, scaled_deep, use
    )
    for chain in range(chains):
        potential[chain] = before[chain] + fold((0.5 * inv_noise) * misfits[chain])


def launch(q, draw, slope, mine, other, base, new_q, new_p, mass, totals):
    chains = q.shape[0]
    for part, (start, offset) in ((mine, base[0]), (other, base[1])):
        for i in range(part.shape[0]):
            for cut in tiles(q.shape[-1]):
                im = part[i, :, cut]
                mass[offset + i, :, cut] = im
                inverse_root = 1.0 / jnp.sqrt(im)
                for chain in range(chains):
                    p = draw[chain, start + i, :, cut] * inverse_root
                    totals[chain] = totals[chain] + im * p * p
                    p = p - (0.5 * step_size) * slope[chain, offset + i, :, cut]
                    new_p[chain, offset + i, :, cut] = p
                    new_q[chain, offset + i, :, cut] = (
                        q[chain, start + i, :, cut] + step_size * im * p
                    )


def send_rims(source, to_a, to_b):
    odd = parity()
    for chain in range(source.shape[0]):
        for i in range(WIDE):
            to_a[chain * WIDE + i] = source[chain, (1 - odd) * WIDE + i]
            to_b[chain * WIDE + i] = source[chain, odd * WIDE + i]


def launch_rim_kernel(q, draw, slope, mine, other, new_q, new_p, mass, kinetic, to_a, to_b):
    core = lax.rem(lax.axis_index("chain"), 2)
    chains, planes = q.shape[:2]
    far = planes - WIDE
    totals = [0.0] * chains
    base = ((core * far, core * WIDE), ((1 - core) * far, (1 - core) * WIDE))
    launch(q, draw, slope, mine, other, base, new_q, new_p, mass, totals)
    for chain in range(chains):
        kinetic[chain] = fold(0.5 * totals[chain])
    send_rims(new_q, to_a, to_b)


def launch_inner_kernel(q, draw, slope, mine, other, before, new_q, new_p, mass, kinetic):
    core = lax.rem(lax.axis_index("chain"), 2)
    chains, planes = q.shape[:2]
    half = planes // 2 - WIDE
    totals = [0.0] * chains
    base = tuple((WIDE + c * half, c * half) for c in (core, 1 - core))
    launch(q, draw, slope, mine, other, base, new_q, new_p, mass, totals)
    for chain in range(chains):
        kinetic[chain] = before[chain] + fold(0.5 * totals[chain])


def leap_inner_kernel(q_rim, q_inner, nu, obs, p, mass, scaled, new_q, new_p, deep, scaled_deep):
    def use(chain, x, cut, v, slope):
        at = x - WIDE
        moment = p[chain, at, :, cut] - step_size * slope
        new_p[chain, at, :, cut] = moment
        new_q[chain, at, :, cut] = v + step_size * mass[at, :, cut] * moment

    interior(parts(q_rim, q_inner), nu, obs, scaled, deep, scaled_deep, use)


def rim_index(x, planes):
    return x if x < WIDE else x - planes + 2 * WIDE


def leap_rim_kernel(
    q_rim, q_inner, from_a, from_b, nu, obs, nu_halo, obs_halo, p, mass, scaled,
    new_q, new_p, to_a, to_b, halo, deep, rim_scaled, scaled_deep,
):
    planes = q_inner.shape[1] + 2 * WIDE
    place_halo(halo, from_a, from_b)

    def use(chain, x, cut, v, slope):
        at = rim_index(x, planes)
        moment = p[chain, at, :, cut] - step_size * slope
        new_p[chain, at, :, cut] = moment
        new_q[chain, at, :, cut] = v + step_size * mass[at, :, cut] * moment

    rims(
        parts(q_rim, q_inner), halo, nu, obs, nu_halo, obs_halo,
        scaled, deep, rim_scaled, scaled_deep, use,
    )
    send_rims(new_q, to_a, to_b)


def run(copies):
    for copy in copies:
        copy.start()
    for copy in copies:
        copy.wait()


def rim_copies(rim, out, sems):
    chains, planes = out.shape[:2]
    copies = []
    for chain in range(chains):
        for side, start in enumerate((0, planes - WIDE)):
            copies.append(
                pltpu.make_async_copy(
                    rim.at[chain, pl.ds(side * WIDE, WIDE)],
                    out.at[chain, pl.ds(start, WIDE)],
                    sems.at[2 * chain + side],
                )
            )
    return copies


def inner_copies(inner, out, sems):
    chains, planes = out.shape[:2]
    return [
        pltpu.make_async_copy(
            inner.at[chain], out.at[chain, pl.ds(WIDE, planes - 2 * WIDE)], sems.at[2 * chains + chain]
        )
        for chain in range(chains)
    ]


def store_kernel(rim, inner, out, token, sems):
    token[...] = jnp.zeros_like(token)
    run(rim_copies(rim, out, sems) + inner_copies(inner, out, sems))


def store_inner_kernel(inner, out, sems):
    run(inner_copies(inner, out, sems))


def last_inner_kernel(q_rim, q_inner, nu, obs, p, mass, scaled, new_p, energy, deep, scaled_deep):
    chains, planes = deep.shape[:2]
    q_at = parts(q_rim, q_inner)
    totals = [0.0] * chains

    def use(chain, x, cut, v, slope):
        at = x - WIDE
        moment = p[chain, at, :, cut] - (0.5 * step_size) * slope
        new_p[chain, at, :, cut] = moment
        totals[chain] = totals[chain] + (0.5 * mass[at, :, cut]) * (moment * moment)

    misfits = interior(q_at, nu, obs, scaled, deep, scaled_deep, use)
    for chain in range(chains):
        squares = 0.0
        for x in range(planes):
            view = q_at(chain, x)
            for cut in tiles(view.shape[-1]):
                v = view[:, cut]
                squares = squares + v * v
        energy[chain] = fold(
            (0.5 * inv_noise) * misfits[chain] + (0.5 * prior_weight) * squares + totals[chain]
        )


def last_rim_kernel(
    cells, q_rim, q_inner, from_a, from_b, nu, obs, nu_halo, obs_halo, p, mass, scaled, energy,
    potential, kinetic, stored, partial_p,
    new_p, rows, halo, deep, rim_scaled, scaled_deep, rim_p, sems,
):
    chains, planes = new_p.shape[:2]
    totals = [0.0] * chains
    place_halo(halo, from_a, from_b)

    def use(chain, x, cut, v, slope):
        at = rim_index(x, planes)
        moment = p[chain, at, :, cut] - (0.5 * step_size) * slope
        rim_p[chain, at, :, cut] = moment
        totals[chain] = totals[chain] + (0.5 * mass[at, :, cut]) * (moment * moment)

    copies = rim_copies(rim_p, new_p, sems)
    misfits = rims(
        parts(q_rim, q_inner), halo, nu, obs, nu_halo, obs_halo,
        scaled, deep, rim_scaled, scaled_deep, use,
        lambda chain, high: copies[2 * chain + high].start(),
    )
    sub = lax.broadcasted_iota(jnp.int32, (8, LANES), 0)
    lane = lax.broadcasted_iota(jnp.int32, (8, LANES), 1)
    mark = jnp.zeros((8, LANES), jnp.float32)
    for chain in range(chains):
        end = energy[chain] + fold((0.5 * inv_noise) * misfits[chain] + totals[chain])
        start = potential[chain] + kinetic[chain]
        for row, tile in enumerate((start, end)):
            mark = jnp.where((sub == row) & (lane == chain), jnp.sum(tile) / cells, mark)
    for i in range(rows.shape[0]):
        rows[i] = mark
    for copy in copies:
        copy.wait()


def local(position, momentum_draw, viscosity, observed):
    chains, planes, depth, across = position.shape
    groups, slabs = lax.axis_size("chain"), lax.axis_size("gx")
    cells = planes * slabs * depth * across
    near = [(i, i ^ 1) for i in range(groups)]
    far = [(i, i ^ 2) for i in range(groups)]
    pair_a = [(i, i ^ 1) for i in range(slabs)]
    pair_b = [(i, (i + 1 if i % 2 else i - 1) % slabs) for i in range(slabs)]
    half = planes // 2
    plane = (depth, across)
    rest = planes - 2 * WIDE
    block = (chains, planes, *plane)
    rim_block = (chains, 2 * WIDE, *plane)
    inner_block = (chains, rest, *plane)
    halo = (2, chains, WIDE, *plane)
    edge = (chains * WIDE, *plane)
    sides = (2, *plane)
    tile = (chains, 8, LANES)
    scaled_shape = (chains, planes - 2, *plane)
    field = (chains, planes + 2 * WIDE, *plane)
    inner_scratch = [block, scaled_shape]
    rim_scratch = [halo, field, rim_block, (chains, planes + 2, *plane)]
    work = chains * planes * depth * across * 30

    def swap(to_a, to_b):
        return lax.ppermute(to_a, "gx", pair_a), lax.ppermute(to_b, "gx", pair_b)

    first_edge = (chains * WIDE + 2, *plane)
    sums = (half, 2, *plane)
    position, keep, send, to_a, to_b = call(
        entry_kernel, [block, sums, sums, first_edge, first_edge],
        [pltpu.SemaphoreType.DMA((chains + 4,))], "entry", work // 16, [MEMORY] * 3,
    )(*(pltpu.with_memory_space_constraint(a, pltpu.HBM) for a in (position, viscosity, observed)))
    from_a, from_b = swap(to_a, to_b)
    got = lax.ppermute(send, "chain", near)

    def mass_body(*refs):
        mass_kernel(chains * groups, *refs)

    def mass_of(count, rim, after, before_mass, name):
        def add_body(*refs):
            add_kernel(rim, *refs)

        part = call(add_body, [(count, 2, *plane)], [], name + "_add", work // 16)(keep, got, *after)[0]
        remote = lax.ppermute(part, "chain", far)
        mine = call(mass_body, [(count, *plane)], [], name, work // 16)(part, remote, *before_mass)[0]
        return mine, lax.ppermute(mine, "chain", near)

    scaled, inner_slope, potential = call(
        first_inner_kernel, [scaled_shape, inner_block, tile], inner_scratch, "first_inner", work
    )(position, viscosity, observed)
    mine, other = mass_of(WIDE, True, (), (potential,), "mass_rim")
    inner_mine, inner_other = mass_of(half - WIDE, False, (), (), "mass_inner")
    slope, nu_halo, obs_halo, potential = call(
        first_rim_kernel, [rim_block, sides, sides, tile], rim_scratch, "first_rim", work
    )(position, from_a, from_b, viscosity, observed, scaled, potential)
    rim_q, rim_p, rim_mass, kinetic, to_a, to_b = call(
        launch_rim_kernel,
        [rim_block, rim_block, (2 * WIDE, *plane), tile, edge, edge],
        [], "launch_rim", work // 4,
    )(position, momentum_draw, slope, mine, other)
    from_a, from_b = swap(to_a, to_b)
    inner_q, inner_p, inner_mass, kinetic = call(
        launch_inner_kernel,
        [inner_block, inner_block, (rest, *plane), tile],
        [], "launch_inner", work // 4,
    )(position, momentum_draw, inner_slope, inner_mine, inner_other, kinetic)
    for _ in range(LEAPS - 1):
        old_rim, old_inner = rim_q, inner_q
        scaled, inner_q, inner_p = call(
            leap_inner_kernel, [scaled_shape, inner_block, inner_block], inner_scratch, "leap_inner", work
        )(old_rim, old_inner, viscosity, observed, inner_p, inner_mass)
        rim_q, rim_p, to_a, to_b = call(
            leap_rim_kernel, [rim_block, rim_block, edge, edge], rim_scratch, "leap_rim", work
        )(
            old_rim, old_inner, from_a, from_b, viscosity, observed, nu_halo, obs_halo,
            rim_p, rim_mass, scaled,
        )
        from_a, from_b = swap(to_a, to_b)
    copy_sems = pltpu.SemaphoreType.DMA((3 * chains,))
    q, stored = call(
        store_kernel, [block, (8, LANES)], [copy_sems], "store_q", work // 8, outs=[MEMORY, VECTOR]
    )(rim_q, inner_q)
    scaled, inner_p, energy = call(
        last_inner_kernel, [scaled_shape, inner_block, tile], inner_scratch, "last_inner", work
    )(rim_q, inner_q, viscosity, observed, inner_p, inner_mass)
    partial_p = call(
        store_inner_kernel, [block], [copy_sems], "store_p", work // 16, outs=[MEMORY]
    )(inner_p)[0]

    def last_body(*refs):
        last_rim_kernel(cells, *refs)

    operands = (
        rim_q, inner_q, from_a, from_b, viscosity, observed, nu_halo, obs_halo, rim_p, rim_mass,
        scaled, energy, potential, kinetic, stored, partial_p,
    )
    p, rows = call(
        last_body, [block, (slabs, 8, LANES)], [*rim_scratch, rim_block, copy_sems], "last_rim", work,
        [VECTOR] * (len(operands) - 1) + [MEMORY], [MEMORY, VECTOR], {len(operands) - 1: 0},
    )(*operands)
    rows = lax.all_to_all(rows, "gx", 0, 0, tiled=True)
    energies = jnp.sum(rows[:, :2, :chains], axis=0)
    return (q, p, energies)


def solution(mesh):
    in_specs = (
        P("chain", "gx", None, None),
        P("chain", "gx", None, None),
        P("gx", None, None),
        P("gx", None, None),
    )
    out_specs = (P("chain", "gx", None, None), P("chain", "gx", None, None), P(None, "chain"))
    return jax.shard_map(local, mesh=mesh, in_specs=in_specs, out_specs=out_specs, check_vma=False)
```

```python
import jax
import jax.numpy as jnp
from jax import lax
from jax.experimental import pallas as pl
from jax.experimental.pallas import tpu as pltpu
from jax.sharding import PartitionSpec as P

LEAPS = 2

unit = -0.05
inv_noise = 0.25
prior_weight = 0.5
step_size = 0.05
LANES = 128
WIDE = 2


VECTOR = pl.BlockSpec(memory_space=pltpu.VMEM)
MEMORY = pl.BlockSpec(memory_space=pltpu.HBM)


def call(kernel, out_shapes, scratch, name, work, ins=None, outs=None, aliases=None, limit=32):
    more = {} if ins is None else {"in_specs": ins}
    if aliases:
        more["input_output_aliases"] = aliases
    return pl.pallas_call(
        kernel,
        out_shape=[jax.ShapeDtypeStruct(shape, jnp.float32) for shape in out_shapes],
        out_specs=outs or [VECTOR] * len(out_shapes),
        scratch_shapes=[
            pltpu.VMEM(shape, jnp.float32) if isinstance(shape, tuple) else shape
            for shape in scratch
        ],
        compiler_params=pltpu.CompilerParams(vmem_limit_bytes=limit << 20),
        cost_estimate=pl.CostEstimate(flops=work, bytes_accessed=work // 8, transcendentals=0),
        name=name,
        **more,
    )


def tiles(width):
    return [slice(j * LANES, (j + 1) * LANES) for j in range(width // LANES)]


def depth_sum(v):
    depth = v.shape[0]
    row = lax.broadcasted_iota(jnp.int32, v.shape, 0)
    below = jnp.where(row == 0, 0.0, pltpu.roll(v, 1, 0))
    above = jnp.where(row == depth - 1, 0.0, pltpu.roll(v, depth - 1, 0))
    return below + above


def stencil(planes, deeps):
    cuts = tiles(planes[1].shape[-1])
    edge_terms, own_terms = [], []
    for cut in cuts:
        v = planes[1][:, cut]
        w = deeps[1][:, cut] + (planes[0][:, cut] + planes[2][:, cut])
        corner = deeps[0][:, cut] + deeps[2][:, cut]
        t = 6.0 * v + (2.0 * w + corner)
        d = t + w
        edge_terms.append(t)
        own_terms.append((d + d) - 92.0 * v)
    lane = lax.broadcasted_iota(jnp.int32, edge_terms[0].shape, 1)
    ups = [pltpu.roll(t, 1, 1) for t in edge_terms]
    downs = [pltpu.roll(t, LANES - 1, 1) for t in edge_terms]
    result = []
    for j in range(len(cuts)):
        before = ups[j - 1] if j else 0.0
        after = downs[j + 1] if j + 1 < len(cuts) else 0.0
        left = jnp.where(lane == 0, before, ups[j])
        right = jnp.where(lane == LANES - 1, after, downs[j])
        result.append(own_terms[j] + (left + right))
    return list(zip(cuts, result, strict=True))


def deepen(deep, source):
    for cut in tiles(source.shape[-1]):
        deep[:, cut] = depth_sum(source[:, cut])


def weigh(view, deep, nu, target, out, out_deep):
    total = 0.0
    for cut, k in stencil(view, deep):
        n = nu[:, cut]
        misfit = (unit * n) * k - target[:, cut]
        s = n * misfit
        out[:, cut] = s
        out_deep[:, cut] = depth_sum(s)
        total = total + misfit * misfit
    return total


def fold(total):
    return total[:8] + total[8:]


def whole(q):
    return lambda chain, x: q.at[chain, x]


def parts(rim, inner):
    planes = inner.shape[1] + 2 * WIDE

    def at(chain, x):
        if x < WIDE:
            return rim.at[chain, x]
        if x >= planes - WIDE:
            return rim.at[chain, x - planes + 2 * WIDE]
        return inner.at[chain, x - WIDE]

    return at


def interior(q_at, nu, obs, scaled, deep, scaled_deep, use):
    chains, planes = deep.shape[:2]
    totals = []
    for chain in range(chains):
        for x in range(planes):
            deepen(deep.at[chain, x], q_at(chain, x))
    for chain in range(chains):
        total = 0.0
        for x in range(1, planes - 1):
            near = range(x - 1, x + 2)
            total = total + weigh(
                [q_at(chain, i) for i in near],
                [deep.at[chain, i] for i in near],
                nu.at[x],
                obs.at[x],
                scaled.at[chain, x - 1],
                scaled_deep.at[chain, x - 1],
            )
        totals.append(total)
    for chain in range(chains):
        for x in range(2, planes - 2):
            near = range(x - 2, x + 1)
            view = [scaled.at[chain, i] for i in near]
            for cut, k in stencil(view, [scaled_deep.at[chain, i] for i in near]):
                v = q_at(chain, x)[:, cut]
                use(chain, x, cut, v, (inv_noise * unit) * k + prior_weight * v)
    return totals


def parity():
    return 1 - lax.rem(lax.axis_index("gx"), 2)


def place_halo(halo, from_a, from_b):
    odd = parity()
    chains = halo.shape[1]
    for chain in range(chains):
        for i in range(WIDE):
            halo[1 - odd, chain, i] = from_a[chain * WIDE + i]
            halo[odd, chain, i] = from_b[chain * WIDE + i]


def rims(
    q_at, halo, nu, obs, nu_halo, obs_halo, scaled, deep, rim_scaled, scaled_deep, use, ready=None
):
    chains, planes = scaled.shape[0], scaled.shape[1] + 2

    def at(chain, x):
        if x < 0:
            return halo.at[0, chain, WIDE + x]
        if x >= planes:
            return halo.at[1, chain, x - planes]
        return q_at(chain, x)

    def scaled_at(chain, x):
        if x in (-1, 0):
            return rim_scaled.at[chain, x + 1]
        if x in (planes - 1, planes):
            return rim_scaled.at[chain, x - planes + 3]
        return scaled.at[chain, x - 1]

    sides = ((-2, -1, 0, 1), (planes + 1, planes, planes - 1, planes - 2))
    totals = []
    for chain in range(chains):
        for side in sides:
            for x in side:
                deepen(deep.at[chain, x + WIDE], at(chain, x))
    for chain in range(chains):
        total = 0.0
        for s, side in enumerate(sides):
            for x in side[1:3]:
                outer = x == side[1]
                near = range(x - 1, x + 2)
                squares = weigh(
                    [at(chain, i) for i in near],
                    [deep.at[chain, i + WIDE] for i in near],
                    nu_halo.at[s] if outer else nu.at[x],
                    obs_halo.at[s] if outer else obs.at[x],
                    scaled_at(chain, x),
                    scaled_deep.at[chain, x + 1],
                )
                total = total if outer else total + squares
            for x in (1, 2) if s == 0 else (planes - 2, planes - 3):
                deepen(scaled_deep.at[chain, x + 1], scaled_at(chain, x))
        totals.append(total)
    for chain in range(chains):
        for x in (0, 1, planes - 2, planes - 1):
            near = range(x - 1, x + 2)
            view = [scaled_at(chain, i) for i in near]
            for cut, k in stencil(view, [scaled_deep.at[chain, i + 1] for i in near]):
                v = q_at(chain, x)[:, cut]
                use(chain, x, cut, v, (inv_noise * unit) * k + prior_weight * v)
            if ready and x in (1, planes - 1):
                ready(chain, x > 1)
    return totals


def entry_kernel(q, nu, obs, own, keep, send, to_a, to_b, sems):
    core, odd = lax.rem(lax.axis_index("chain"), 2), parity()
    chains, planes = own.shape[:2]
    half = planes // 2
    load = [pltpu.make_async_copy(q.at[chain], own.at[chain], sems.at[chain]) for chain in range(chains)]
    edges = []
    for i, (source, at) in enumerate(((nu, chains * WIDE), (obs, chains * WIDE + 1))):
        for k, (out, low) in enumerate(((to_a, odd), (to_b, 1 - odd))):
            edges.append(
                pltpu.make_async_copy(
                    source.at[(1 - low) * (planes - 1)], out.at[at], sems.at[chains + 2 * i + k]
                )
            )
    for copy in load + edges:
        copy.start()
    for copy in load:
        copy.wait()
    for chain in range(chains):
        for i in range(WIDE):
            to_a[chain * WIDE + i] = own[chain, (1 - odd) * (planes - WIDE) + i]
            to_b[chain * WIDE + i] = own[chain, odd * (planes - WIDE) + i]
    for x in range(half):
        for out, base in ((keep, core * half), (send, (1 - core) * half)):
            for cut in tiles(own.shape[-1]):
                first = own[0, base + x, :, cut]
                second = first * first
                for chain in range(1, chains):
                    v = own[chain, base + x, :, cut]
                    first = first + v
                    second = second + v * v
                out[x, 0, :, cut] = first
                out[x, 1, :, cut] = second
    for copy in edges:
        copy.wait()


def add_kernel(rim, a, b, *rest):
    core = lax.rem(lax.axis_index("chain"), 2)
    out = rest[-1]
    count = out.shape[0]
    for x in range(count):
        at = (core if rim else 1 - core) * count + x
        out[x] = a[at] + b[at]


def mass_kernel(count, a, b, *rest):
    out = rest[-1]
    for x in range(a.shape[0]):
        mean = (a[x, 0] + b[x, 0]) / count
        out[x] = 0.5 + (a[x, 1] + b[x, 1]) / count - mean * mean


def first_inner_kernel(q, nu, obs, scaled, slope, potential, deep, scaled_deep):
    chains, planes = q.shape[:2]

    def use(chain, x, cut, v, value):
        slope[chain, x - 2, :, cut] = value

    misfits = interior(whole(q), nu, obs, scaled, deep, scaled_deep, use)
    for chain in range(chains):
        squares = 0.0
        for x in range(planes):
            for cut in tiles(q.shape[-1]):
                v = q[chain, x, :, cut]
                squares = squares + v * v
        potential[chain] = fold(
            (0.5 * inv_noise) * misfits[chain] + (0.5 * prior_weight) * squares
        )


def first_rim_kernel(
    q, from_a, from_b, nu, obs, scaled, before,
    slope, nu_halo, obs_halo, potential, halo, deep, rim_scaled, scaled_deep,
):
    odd = parity()
    chains, planes = q.shape[:2]
    place_halo(halo, from_a, from_b)
    for out, at in ((nu_halo, chains * WIDE), (obs_halo, chains * WIDE + 1)):
        out[1 - odd] = from_a[at]
        out[odd] = from_b[at]

    def use(chain, x, cut, v, value):
        slope[chain, x if x < 2 else x - planes + 4, :, cut] = value

    misfits = rims(
        whole(q), halo, nu, obs, nu_halo, obs_halo, scaled, deep, rim_scaled, scaled_deep, use
    )
    for chain in range(chains):
        potential[chain] = before[chain] + fold((0.5 * inv_noise) * misfits[chain])


def launch(q, draw, slope, mine, other, base, new_q, new_p, mass, totals):
    chains = q.shape[0]
    for part, (start, offset) in ((mine, base[0]), (other, base[1])):
        for i in range(part.shape[0]):
            for cut in tiles(q.shape[-1]):
                im = part[i, :, cut]
                mass[offset + i, :, cut] = im
                inverse_root = 1.0 / jnp.sqrt(im)
                for chain in range(chains):
                    p = draw[chain, start + i, :, cut] * inverse_root
                    totals[chain] = totals[chain] + im * p * p
                    p = p - (0.5 * step_size) * slope[chain, offset + i, :, cut]
                    new_p[chain, offset + i, :, cut] = p
                    new_q[chain, offset + i, :, cut] = (
                        q[chain, start + i, :, cut] + step_size * im * p
                    )


def send_rims(source, to_a, to_b):
    odd = parity()
    for chain in range(source.shape[0]):
        for i in range(WIDE):
            to_a[chain * WIDE + i] = source[chain, (1 - odd) * WIDE + i]
            to_b[chain * WIDE + i] = source[chain, odd * WIDE + i]


def launch_rim_kernel(q, draw, slope, mine, other, new_q, new_p, mass, kinetic, to_a, to_b):
    core = lax.rem(lax.axis_index("chain"), 2)
    chains, planes = q.shape[:2]
    far = planes - WIDE
    totals = [0.0] * chains
    base = ((core * far, core * WIDE), ((1 - core) * far, (1 - core) * WIDE))
    launch(q, draw, slope, mine, other, base, new_q, new_p, mass, totals)
    for chain in range(chains):
        kinetic[chain] = fold(0.5 * totals[chain])
    send_rims(new_q, to_a, to_b)


def launch_inner_kernel(q, draw, slope, mine, other, before, new_q, new_p, mass, kinetic):
    core = lax.rem(lax.axis_index("chain"), 2)
    chains, planes = q.shape[:2]
    half = planes // 2 - WIDE
    totals = [0.0] * chains
    base = tuple((WIDE + c * half, c * half) for c in (core, 1 - core))
    launch(q, draw, slope, mine, other, base, new_q, new_p, mass, totals)
    for chain in range(chains):
        kinetic[chain] = before[chain] + fold(0.5 * totals[chain])


def leap_inner_kernel(q_rim, q_inner, nu, obs, p, mass, scaled, new_q, new_p, deep, scaled_deep):
    def use(chain, x, cut, v, slope):
        at = x - WIDE
        moment = p[chain, at, :, cut] - step_size * slope
        new_p[chain, at, :, cut] = moment
        new_q[chain, at, :, cut] = v + step_size * mass[at, :, cut] * moment

    interior(parts(q_rim, q_inner), nu, obs, scaled, deep, scaled_deep, use)


def rim_index(x, planes):
    return x if x < WIDE else x - planes + 2 * WIDE


def leap_rim_kernel(
    q_rim, q_inner, from_a, from_b, nu, obs, nu_halo, obs_halo, p, mass, scaled,
    new_q, new_p, to_a, to_b, halo, deep, rim_scaled, scaled_deep,
):
    planes = q_inner.shape[1] + 2 * WIDE
    place_halo(halo, from_a, from_b)

    def use(chain, x, cut, v, slope):
        at = rim_index(x, planes)
        moment = p[chain, at, :, cut] - step_size * slope
        new_p[chain, at, :, cut] = moment
        new_q[chain, at, :, cut] = v + step_size * mass[at, :, cut] * moment

    rims(
        parts(q_rim, q_inner), halo, nu, obs, nu_halo, obs_halo,
        scaled, deep, rim_scaled, scaled_deep, use,
    )
    send_rims(new_q, to_a, to_b)


def run(copies):
    for copy in copies:
        copy.start()
    for copy in copies:
        copy.wait()


def rim_copies(rim, out, sems):
    chains, planes = out.shape[:2]
    copies = []
    for chain in range(chains):
        for side, start in enumerate((0, planes - WIDE)):
            copies.append(
                pltpu.make_async_copy(
                    rim.at[chain, pl.ds(side * WIDE, WIDE)],
                    out.at[chain, pl.ds(start, WIDE)],
                    sems.at[2 * chain + side],
                )
            )
    return copies


def inner_copies(inner, out, sems):
    chains, planes = out.shape[:2]
    return [
        pltpu.make_async_copy(
            inner.at[chain], out.at[chain, pl.ds(WIDE, planes - 2 * WIDE)], sems.at[2 * chains + chain]
        )
        for chain in range(chains)
    ]


def store_kernel(rim, inner, out, token, sems):
    token[...] = jnp.zeros_like(token)
    run(rim_copies(rim, out, sems) + inner_copies(inner, out, sems))


def store_inner_kernel(inner, out, sems):
    run(inner_copies(inner, out, sems))


def last_inner_kernel(q_rim, q_inner, nu, obs, p, mass, scaled, new_p, energy, deep, scaled_deep):
    chains, planes = deep.shape[:2]
    q_at = parts(q_rim, q_inner)
    totals = [0.0] * chains

    def use(chain, x, cut, v, slope):
        at = x - WIDE
        moment = p[chain, at, :, cut] - (0.5 * step_size) * slope
        new_p[chain, at, :, cut] = moment
        totals[chain] = totals[chain] + (0.5 * mass[at, :, cut]) * (moment * moment)

    misfits = interior(q_at, nu, obs, scaled, deep, scaled_deep, use)
    for chain in range(chains):
        squares = 0.0
        for x in range(planes):
            view = q_at(chain, x)
            for cut in tiles(view.shape[-1]):
                v = view[:, cut]
                squares = squares + v * v
        energy[chain] = fold(
            (0.5 * inv_noise) * misfits[chain] + (0.5 * prior_weight) * squares + totals[chain]
        )


def last_rim_kernel(
    cells, q_rim, q_inner, from_a, from_b, nu, obs, nu_halo, obs_halo, p, mass, scaled, energy,
    potential, kinetic, stored, partial_p,
    new_p, rows, halo, deep, rim_scaled, scaled_deep, rim_p, sems,
):
    chains, planes = new_p.shape[:2]
    totals = [0.0] * chains
    place_halo(halo, from_a, from_b)

    def use(chain, x, cut, v, slope):
        at = rim_index(x, planes)
        moment = p[chain, at, :, cut] - (0.5 * step_size) * slope
        rim_p[chain, at, :, cut] = moment
        totals[chain] = totals[chain] + (0.5 * mass[at, :, cut]) * (moment * moment)

    copies = rim_copies(rim_p, new_p, sems)
    misfits = rims(
        parts(q_rim, q_inner), halo, nu, obs, nu_halo, obs_halo,
        scaled, deep, rim_scaled, scaled_deep, use,
        lambda chain, high: copies[2 * chain + high].start(),
    )
    lane = lax.broadcasted_iota(jnp.int32, (1, LANES), 1)
    mark = jnp.zeros((1, LANES), jnp.float32)
    for chain in range(chains):
        end = energy[chain] + fold((0.5 * inv_noise) * misfits[chain] + totals[chain])
        start = potential[chain] + kinetic[chain]
        for row, tile in enumerate((start, end)):
            mark = jnp.where(lane == row * chains + chain, jnp.sum(tile) / cells, mark)
    for i in range(rows.shape[0]):
        rows[i] = mark
    for copy in copies:
        copy.wait()


def local(position, momentum_draw, viscosity, observed):
    chains, planes, depth, across = position.shape
    groups, slabs = lax.axis_size("chain"), lax.axis_size("gx")
    cells = planes * slabs * depth * across
    near = [(i, i ^ 1) for i in range(groups)]
    far = [(i, i ^ 2) for i in range(groups)]
    pair_a = [(i, (i + 1 if i % 2 else i - 1) % slabs) for i in range(slabs)]
    pair_b = [(i, i ^ 1) for i in range(slabs)]
    half = planes // 2
    plane = (depth, across)
    rest = planes - 2 * WIDE
    block = (chains, planes, *plane)
    rim_block = (chains, 2 * WIDE, *plane)
    inner_block = (chains, rest, *plane)
    halo = (2, chains, WIDE, *plane)
    edge = (chains * WIDE, *plane)
    sides = (2, *plane)
    tile = (chains, 8, LANES)
    scaled_shape = (chains, planes - 2, *plane)
    field = (chains, planes + 2 * WIDE, *plane)
    inner_scratch = [block, scaled_shape]
    rim_scratch = [halo, field, rim_block, (chains, planes + 2, *plane)]
    work = chains * planes * depth * across * 30

    def swap(to_a, to_b):
        return lax.ppermute(to_a, "gx", pair_a), lax.ppermute(to_b, "gx", pair_b)

    first_edge = (chains * WIDE + 2, *plane)
    sums = (half, 2, *plane)
    position, keep, send, to_a, to_b = call(
        entry_kernel, [block, sums, sums, first_edge, first_edge],
        [pltpu.SemaphoreType.DMA((chains + 4,))], "entry", work // 16, [MEMORY] * 3,
    )(*(pltpu.with_memory_space_constraint(a, pltpu.HBM) for a in (position, viscosity, observed)))
    from_a, from_b = swap(to_a, to_b)
    got = lax.ppermute(send, "chain", near)

    def mass_body(*refs):
        mass_kernel(chains * groups, *refs)

    def mass_of(count, rim, after, before_mass, name):
        def add_body(*refs):
            add_kernel(rim, *refs)

        part = call(add_body, [(count, 2, *plane)], [], name + "_add", work // 16)(keep, got, *after)[0]
        remote = lax.ppermute(part, "chain", far)
        mine = call(mass_body, [(count, *plane)], [], name, work // 16)(part, remote, *before_mass)[0]
        return mine, lax.ppermute(mine, "chain", near)

    scaled, inner_slope, potential = call(
        first_inner_kernel, [scaled_shape, inner_block, tile], inner_scratch, "first_inner", work
    )(position, viscosity, observed)
    mine, other = mass_of(WIDE, True, (), (potential,), "mass_rim")
    slope, nu_halo, obs_halo, potential = call(
        first_rim_kernel, [rim_block, sides, sides, tile], rim_scratch, "first_rim", work
    )(position, from_a, from_b, viscosity, observed, scaled, potential)
    inner_mine, inner_other = mass_of(half - WIDE, False, (slope,), (), "mass_inner")
    rim_q, rim_p, rim_mass, kinetic, to_a, to_b = call(
        launch_rim_kernel,
        [rim_block, rim_block, (2 * WIDE, *plane), tile, edge, edge],
        [], "launch_rim", work // 4,
    )(position, momentum_draw, slope, mine, other)
    from_a, from_b = swap(to_a, to_b)
    inner_q, inner_p, inner_mass, kinetic = call(
        launch_inner_kernel,
        [inner_block, inner_block, (rest, *plane), tile],
        [], "launch_inner", work // 4,
    )(position, momentum_draw, inner_slope, inner_mine, inner_other, kinetic)
    for _ in range(LEAPS - 1):
        old_rim, old_inner = rim_q, inner_q
        scaled, inner_q, inner_p = call(
            leap_inner_kernel, [scaled_shape, inner_block, inner_block], inner_scratch, "leap_inner", work
        )(old_rim, old_inner, viscosity, observed, inner_p, inner_mass)
        rim_q, rim_p, to_a, to_b = call(
            leap_rim_kernel, [rim_block, rim_block, edge, edge], rim_scratch, "leap_rim", work
        )(
            old_rim, old_inner, from_a, from_b, viscosity, observed, nu_halo, obs_halo,
            rim_p, rim_mass, scaled,
        )
        from_a, from_b = swap(to_a, to_b)
    copy_sems = pltpu.SemaphoreType.DMA((3 * chains,))
    q, stored = call(
        store_kernel, [block, (8, LANES)], [copy_sems], "store_q", work // 8, outs=[MEMORY, VECTOR]
    )(rim_q, inner_q)
    scaled, inner_p, energy = call(
        last_inner_kernel, [scaled_shape, inner_block, tile], inner_scratch, "last_inner", work
    )(rim_q, inner_q, viscosity, observed, inner_p, inner_mass)
    partial_p = call(
        store_inner_kernel, [block], [copy_sems], "store_p", work // 16, outs=[MEMORY]
    )(inner_p)[0]

    def last_body(*refs):
        last_rim_kernel(cells, *refs)

    operands = (
        rim_q, inner_q, from_a, from_b, viscosity, observed, nu_halo, obs_halo, rim_p, rim_mass,
        scaled, energy, potential, kinetic, stored, partial_p,
    )
    p, rows = call(
        last_body, [block, (slabs, 1, LANES)], [*rim_scratch, rim_block, copy_sems], "last_rim", work,
        [VECTOR] * (len(operands) - 1) + [MEMORY], [MEMORY, VECTOR], {len(operands) - 1: 0},
    )(*operands)
    rows = lax.all_to_all(rows, "gx", 0, 0, tiled=True)
    energies = jnp.sum(rows[:, 0, : 2 * chains].reshape(slabs, 2, chains), axis=0)
    return (q, p, energies)


def solution(mesh):
    in_specs = (
        P("chain", "gx", None, None),
        P("chain", "gx", None, None),
        P("gx", None, None),
        P("gx", None, None),
    )
    out_specs = (P("chain", "gx", None, None), P("chain", "gx", None, None), P(None, "chain"))
    return jax.shard_map(local, mesh=mesh, in_specs=in_specs, out_specs=out_specs, check_vma=False)
```

```python
import jax
import jax.numpy as jnp
from jax import lax
from jax.experimental import pallas as pl
from jax.experimental.pallas import tpu as pltpu
from jax.sharding import PartitionSpec as P

LEAPS = 2

unit = -0.05
inv_noise = 0.25
prior_weight = 0.5
step_size = 0.05
LANES = 128
WIDE = 2


VECTOR = pl.BlockSpec(memory_space=pltpu.VMEM)
MEMORY = pl.BlockSpec(memory_space=pltpu.HBM)


def call(kernel, out_shapes, scratch, name, work, ins=None, outs=None, aliases=None, limit=32):
    more = {} if ins is None else {"in_specs": ins}
    if aliases:
        more["input_output_aliases"] = aliases
    return pl.pallas_call(
        kernel,
        out_shape=[jax.ShapeDtypeStruct(shape, jnp.float32) for shape in out_shapes],
        out_specs=outs or [VECTOR] * len(out_shapes),
        scratch_shapes=[
            pltpu.VMEM(shape, jnp.float32) if isinstance(shape, tuple) else shape
            for shape in scratch
        ],
        compiler_params=pltpu.CompilerParams(vmem_limit_bytes=limit << 20),
        cost_estimate=pl.CostEstimate(flops=work, bytes_accessed=work // 8, transcendentals=0),
        name=name,
        **more,
    )


def tiles(width):
    return [slice(j * LANES, (j + 1) * LANES) for j in range(width // LANES)]


def depth_sum(v):
    depth = v.shape[0]
    row = lax.broadcasted_iota(jnp.int32, v.shape, 0)
    below = jnp.where(row == 0, 0.0, pltpu.roll(v, 1, 0))
    above = jnp.where(row == depth - 1, 0.0, pltpu.roll(v, depth - 1, 0))
    return below + above


def present(views, cut):
    value = None
    for view in views:
        if view is not None:
            value = view[:, cut] if value is None else value + view[:, cut]
    return value


def stencil(planes, deeps):
    cuts = tiles(planes[2].shape[-1])
    edge_terms, own_terms = [], []
    for cut in cuts:
        v = 0.0 if planes[1] is None else planes[1][:, cut]
        w = present([deeps[1], planes[0], planes[2]], cut)
        corner = present([deeps[0], deeps[2]], cut)
        t = 6.0 * v + (2.0 * w + corner)
        d = t + w
        edge_terms.append(t)
        own_terms.append((d + d) - 92.0 * v)
    lane = lax.broadcasted_iota(jnp.int32, edge_terms[0].shape, 1)
    ups = [pltpu.roll(t, 1, 1) for t in edge_terms]
    downs = [pltpu.roll(t, LANES - 1, 1) for t in edge_terms]
    result = []
    for j in range(len(cuts)):
        before = ups[j - 1] if j else 0.0
        after = downs[j + 1] if j + 1 < len(cuts) else 0.0
        left = jnp.where(lane == 0, before, ups[j])
        right = jnp.where(lane == LANES - 1, after, downs[j])
        result.append(own_terms[j] + (left + right))
    return list(zip(cuts, result, strict=True))


def deepen(deep, source):
    for cut in tiles(source.shape[-1]):
        deep[:, cut] = depth_sum(source[:, cut])


def weigh(view, deep, nu, target, out, out_deep):
    total = 0.0
    for cut, k in stencil(view, deep):
        n = nu[:, cut]
        misfit = (unit * n) * k - target[:, cut]
        s = n * misfit
        out[:, cut] = s
        out_deep[:, cut] = depth_sum(s)
        total = total + misfit * misfit
    return total


def fold(total):
    return total[:8] + total[8:]


def whole(q):
    return lambda chain, x: q.at[chain, x]


def parts(rim, inner):
    planes = inner.shape[1] + 2 * WIDE

    def at(chain, x):
        if x < WIDE:
            return rim.at[chain, x]
        if x >= planes - WIDE:
            return rim.at[chain, x - planes + 2 * WIDE]
        return inner.at[chain, x - WIDE]

    return at


def interior(q_at, nu, obs, scaled, deep, scaled_deep, use):
    chains, planes = deep.shape[:2]
    totals = []
    for chain in range(chains):
        for x in range(planes):
            deepen(deep.at[chain, x], q_at(chain, x))
    for chain in range(chains):
        total = 0.0
        for x in range(1, planes - 1):
            near = range(x - 1, x + 2)
            total = total + weigh(
                [q_at(chain, i) for i in near],
                [deep.at[chain, i] for i in near],
                nu.at[x],
                obs.at[x],
                scaled.at[chain, x - 1],
                scaled_deep.at[chain, x - 1],
            )
        totals.append(total)
    for chain in range(chains):
        for x in range(2, planes - 2):
            near = range(x - 2, x + 1)
            view = [scaled.at[chain, i] for i in near]
            for cut, k in stencil(view, [scaled_deep.at[chain, i] for i in near]):
                v = q_at(chain, x)[:, cut]
                use(chain, x, cut, v, (inv_noise * unit) * k + prior_weight * v)
    return totals


def parity():
    return 1 - lax.rem(lax.axis_index("gx"), 2)


def place_halo(halo, from_a, from_b):
    odd = parity()
    chains = halo.shape[1]
    for chain in range(chains):
        for i in range(WIDE):
            halo[1 - odd, chain, i] = from_a[chain * WIDE + i]
            halo[odd, chain, i] = from_b[chain * WIDE + i]


def rims(
    q_at, halo, nu, obs, nu_halo, scaled, deep, rim_scaled, scaled_deep, use, ready=None
):
    chains, planes = scaled.shape[0], scaled.shape[1] + 2

    def at(chain, x):
        if x < 0:
            return halo.at[0, chain, 0]
        if x >= planes:
            return halo.at[1, chain, 0]
        return q_at(chain, x)

    def scaled_at(chain, x):
        if x in (-1, 0):
            return rim_scaled.at[chain, x + 1]
        if x in (planes - 1, planes):
            return rim_scaled.at[chain, x - planes + 3]
        return scaled.at[chain, x - 1]

    sides = ((-1, 0, 1), (planes, planes - 1, planes - 2))
    totals = []
    for chain in range(chains):
        for side in sides:
            for x in side:
                deepen(deep.at[chain, x + WIDE], at(chain, x))
    for chain in range(chains):
        total = 0.0
        for s, (outer, x, _) in enumerate(sides):
            view = [None, None, at(chain, x)]
            for cut, k in stencil(view, [None, None, deep.at[chain, x + WIDE]]):
                n = nu_halo[s, :, cut]
                value = (unit * n * n) * k + halo[s, chain, 1, :, cut]
                scaled_at(chain, outer)[:, cut] = value
                scaled_deep[chain, outer + 1, :, cut] = depth_sum(value)
            near = range(x - 1, x + 2)
            total = total + weigh(
                [at(chain, i) for i in near],
                [deep.at[chain, i + WIDE] for i in near],
                nu.at[x],
                obs.at[x],
                scaled_at(chain, x),
                scaled_deep.at[chain, x + 1],
            )
            for x in (1, 2) if s == 0 else (planes - 2, planes - 3):
                deepen(scaled_deep.at[chain, x + 1], scaled_at(chain, x))
        totals.append(total)
    for chain in range(chains):
        for x in (0, 1, planes - 2, planes - 1):
            near = range(x - 1, x + 2)
            view = [scaled_at(chain, i) for i in near]
            for cut, k in stencil(view, [scaled_deep.at[chain, i + 1] for i in near]):
                v = q_at(chain, x)[:, cut]
                use(chain, x, cut, v, (inv_noise * unit) * k + prior_weight * v)
            if ready and x in (1, planes - 1):
                ready(chain, x > 1)
    return totals


def entry_kernel(q, nu, obs, own, keep, send, to_a, to_b, edges, deep, known, sems):
    core, odd = lax.rem(lax.axis_index("chain"), 2), parity()
    chains, planes = own.shape[:2]
    half = planes // 2
    load = [pltpu.make_async_copy(q.at[chain], own.at[chain], sems.at[chain]) for chain in range(chains)]
    for i, source in enumerate((nu, obs)):
        for side in range(2):
            at = 2 * i + side
            load.append(
                pltpu.make_async_copy(source.at[side * (planes - 1)], edges.at[at], sems.at[chains + at])
            )
    for copy in load:
        copy.start()
    for copy in load:
        copy.wait()
    near = (0, 1, planes - 2, planes - 1)
    send_rims(
        lambda chain, i: own.at[chain, near[i]],
        (edges.at[0], edges.at[1]), (edges.at[2], edges.at[3]), to_a, to_b, deep, known,
    )
    for chain in range(chains):
        to_a[2 * chain] = own[chain, (1 - odd) * (planes - 1)]
        to_b[2 * chain] = own[chain, odd * (planes - 1)]
    to_a[2 * chains] = edges[1 - odd]
    to_b[2 * chains] = edges[odd]
    for x in range(half):
        for out, base in ((keep, core * half), (send, (1 - core) * half)):
            for cut in tiles(own.shape[-1]):
                first = own[0, base + x, :, cut]
                second = first * first
                for chain in range(1, chains):
                    v = own[chain, base + x, :, cut]
                    first = first + v
                    second = second + v * v
                out[x, 0, :, cut] = first
                out[x, 1, :, cut] = second


def add_kernel(rim, a, b, *rest):
    core = lax.rem(lax.axis_index("chain"), 2)
    out = rest[-1]
    count = out.shape[0]
    for x in range(count):
        at = (core if rim else 1 - core) * count + x
        out[x] = a[at] + b[at]


def mass_kernel(count, a, b, *rest):
    out = rest[-1]
    for x in range(a.shape[0]):
        mean = (a[x, 0] + b[x, 0]) / count
        out[x] = 0.5 + (a[x, 1] + b[x, 1]) / count - mean * mean


def first_inner_kernel(q, nu, obs, scaled, slope, potential, deep, scaled_deep):
    chains, planes = q.shape[:2]

    def use(chain, x, cut, v, value):
        slope[chain, x - 2, :, cut] = value

    misfits = interior(whole(q), nu, obs, scaled, deep, scaled_deep, use)
    for chain in range(chains):
        squares = 0.0
        for x in range(planes):
            for cut in tiles(q.shape[-1]):
                v = q[chain, x, :, cut]
                squares = squares + v * v
        potential[chain] = fold(
            (0.5 * inv_noise) * misfits[chain] + (0.5 * prior_weight) * squares
        )


def first_rim_kernel(
    q, from_a, from_b, nu, obs, scaled, before,
    slope, nu_halo, potential, halo, deep, rim_scaled, scaled_deep,
):
    odd = parity()
    chains, planes = q.shape[:2]
    place_halo(halo, from_a, from_b)
    nu_halo[1 - odd] = from_a[chains * WIDE]
    nu_halo[odd] = from_b[chains * WIDE]

    def use(chain, x, cut, v, value):
        slope[chain, x if x < 2 else x - planes + 4, :, cut] = value

    misfits = rims(
        whole(q), halo, nu, obs, nu_halo, scaled, deep, rim_scaled, scaled_deep, use
    )
    for chain in range(chains):
        potential[chain] = before[chain] + fold((0.5 * inv_noise) * misfits[chain])


def launch(q, draw, slope, mine, other, base, new_q, new_p, mass, totals):
    chains = q.shape[0]
    for part, (start, offset) in ((mine, base[0]), (other, base[1])):
        for i in range(part.shape[0]):
            for cut in tiles(q.shape[-1]):
                im = part[i, :, cut]
                mass[offset + i, :, cut] = im
                inverse_root = 1.0 / jnp.sqrt(im)
                for chain in range(chains):
                    p = draw[chain, start + i, :, cut] * inverse_root
                    totals[chain] = totals[chain] + im * p * p
                    p = p - (0.5 * step_size) * slope[chain, offset + i, :, cut]
                    new_p[chain, offset + i, :, cut] = p
                    new_q[chain, offset + i, :, cut] = (
                        q[chain, start + i, :, cut] + step_size * im * p
                    )


def send_rims(rim, nu_edges, obs_edges, to_a, to_b, deep, known):
    odd = parity()
    chains = deep.shape[0]
    for chain in range(chains):
        for i in range(2 * WIDE):
            deepen(deep.at[chain, i], rim(chain, i))
        for side, (edge, inside) in enumerate(((0, 1), (3, 2))):
            view = [None, rim(chain, edge), rim(chain, inside)]
            for cut, k in stencil(view, [None, deep.at[chain, edge], deep.at[chain, inside]]):
                n = nu_edges[side][:, cut]
                known[side, chain, :, cut] = n * ((unit * n) * k - obs_edges[side][:, cut])
        to_a[2 * chain + 1] = known[1 - odd, chain]
        to_b[2 * chain + 1] = known[odd, chain]


def edges_of(field):
    return field.at[0], field.at[field.shape[0] - 1]


def send_new_rims(new_q, nu, obs, to_a, to_b, deep, known):
    odd = parity()
    send_rims(
        lambda chain, i: new_q.at[chain, i], edges_of(nu), edges_of(obs), to_a, to_b, deep, known
    )
    for chain in range(deep.shape[0]):
        to_a[2 * chain] = new_q[chain, (1 - odd) * 3]
        to_b[2 * chain] = new_q[chain, odd * 3]


def launch_rim_kernel(
    q, draw, slope, mine, other, nu, obs, new_q, new_p, mass, kinetic, to_a, to_b, deep, known
):
    core = lax.rem(lax.axis_index("chain"), 2)
    chains, planes = q.shape[:2]
    far = planes - WIDE
    totals = [0.0] * chains
    base = ((core * far, core * WIDE), ((1 - core) * far, (1 - core) * WIDE))
    launch(q, draw, slope, mine, other, base, new_q, new_p, mass, totals)
    for chain in range(chains):
        kinetic[chain] = fold(0.5 * totals[chain])
    send_new_rims(new_q, nu, obs, to_a, to_b, deep, known)


def launch_inner_kernel(q, draw, slope, mine, other, before, new_q, new_p, mass, kinetic):
    core = lax.rem(lax.axis_index("chain"), 2)
    chains, planes = q.shape[:2]
    half = planes // 2 - WIDE
    totals = [0.0] * chains
    base = tuple((WIDE + c * half, c * half) for c in (core, 1 - core))
    launch(q, draw, slope, mine, other, base, new_q, new_p, mass, totals)
    for chain in range(chains):
        kinetic[chain] = before[chain] + fold(0.5 * totals[chain])


def leap_inner_kernel(q_rim, q_inner, nu, obs, p, mass, scaled, new_q, new_p, deep, scaled_deep):
    def use(chain, x, cut, v, slope):
        at = x - WIDE
        moment = p[chain, at, :, cut] - step_size * slope
        new_p[chain, at, :, cut] = moment
        new_q[chain, at, :, cut] = v + step_size * mass[at, :, cut] * moment

    interior(parts(q_rim, q_inner), nu, obs, scaled, deep, scaled_deep, use)


def rim_index(x, planes):
    return x if x < WIDE else x - planes + 2 * WIDE


def leap_rim_kernel(
    q_rim, q_inner, from_a, from_b, nu, obs, nu_halo, p, mass, scaled,
    new_q, new_p, to_a, to_b, halo, deep, rim_scaled, scaled_deep, send_deep, known,
):
    planes = q_inner.shape[1] + 2 * WIDE
    place_halo(halo, from_a, from_b)

    def use(chain, x, cut, v, slope):
        at = rim_index(x, planes)
        moment = p[chain, at, :, cut] - step_size * slope
        new_p[chain, at, :, cut] = moment
        new_q[chain, at, :, cut] = v + step_size * mass[at, :, cut] * moment

    rims(
        parts(q_rim, q_inner), halo, nu, obs, nu_halo,
        scaled, deep, rim_scaled, scaled_deep, use,
    )
    send_new_rims(new_q, nu, obs, to_a, to_b, send_deep, known)


def run(copies):
    for copy in copies:
        copy.start()
    for copy in copies:
        copy.wait()


def rim_copies(rim, out, sems):
    chains, planes = out.shape[:2]
    copies = []
    for chain in range(chains):
        for side, start in enumerate((0, planes - WIDE)):
            copies.append(
                pltpu.make_async_copy(
                    rim.at[chain, pl.ds(side * WIDE, WIDE)],
                    out.at[chain, pl.ds(start, WIDE)],
                    sems.at[2 * chain + side],
                )
            )
    return copies


def inner_copies(inner, out, sems):
    chains, planes = out.shape[:2]
    return [
        pltpu.make_async_copy(
            inner.at[chain], out.at[chain, pl.ds(WIDE, planes - 2 * WIDE)], sems.at[2 * chains + chain]
        )
        for chain in range(chains)
    ]


def store_kernel(rim, inner, out, token, sems):
    token[...] = jnp.zeros_like(token)
    run(rim_copies(rim, out, sems) + inner_copies(inner, out, sems))


def store_inner_kernel(inner, out, sems):
    run(inner_copies(inner, out, sems))


def last_inner_kernel(q_rim, q_inner, nu, obs, p, mass, scaled, new_p, energy, deep, scaled_deep):
    chains, planes = deep.shape[:2]
    q_at = parts(q_rim, q_inner)
    totals = [0.0] * chains

    def use(chain, x, cut, v, slope):
        at = x - WIDE
        moment = p[chain, at, :, cut] - (0.5 * step_size) * slope
        new_p[chain, at, :, cut] = moment
        totals[chain] = totals[chain] + (0.5 * mass[at, :, cut]) * (moment * moment)

    misfits = interior(q_at, nu, obs, scaled, deep, scaled_deep, use)
    for chain in range(chains):
        squares = 0.0
        for x in range(planes):
            view = q_at(chain, x)
            for cut in tiles(view.shape[-1]):
                v = view[:, cut]
                squares = squares + v * v
        energy[chain] = fold(
            (0.5 * inv_noise) * misfits[chain] + (0.5 * prior_weight) * squares + totals[chain]
        )


def last_rim_kernel(
    cells, q_rim, q_inner, from_a, from_b, nu, obs, nu_halo, p, mass, scaled, energy,
    potential, kinetic, stored, partial_p,
    new_p, rows, halo, deep, rim_scaled, scaled_deep, rim_p, sems,
):
    chains, planes = new_p.shape[:2]
    totals = [0.0] * chains
    place_halo(halo, from_a, from_b)

    def use(chain, x, cut, v, slope):
        at = rim_index(x, planes)
        moment = p[chain, at, :, cut] - (0.5 * step_size) * slope
        rim_p[chain, at, :, cut] = moment
        totals[chain] = totals[chain] + (0.5 * mass[at, :, cut]) * (moment * moment)

    copies = rim_copies(rim_p, new_p, sems)
    misfits = rims(
        parts(q_rim, q_inner), halo, nu, obs, nu_halo,
        scaled, deep, rim_scaled, scaled_deep, use,
        lambda chain, high: copies[2 * chain + high].start(),
    )
    lane = lax.broadcasted_iota(jnp.int32, (1, LANES), 1)
    mark = jnp.zeros((1, LANES), jnp.float32)
    for chain in range(chains):
        end = energy[chain] + fold((0.5 * inv_noise) * misfits[chain] + totals[chain])
        start = potential[chain] + kinetic[chain]
        for row, tile in enumerate((start, end)):
            mark = jnp.where(lane == row * chains + chain, jnp.sum(tile) / cells, mark)
    for i in range(rows.shape[0]):
        rows[i] = mark
    for copy in copies:
        copy.wait()


def local(position, momentum_draw, viscosity, observed):
    chains, planes, depth, across = position.shape
    groups, slabs = lax.axis_size("chain"), lax.axis_size("gx")
    cells = planes * slabs * depth * across
    near = [(i, i ^ 1) for i in range(groups)]
    far = [(i, i ^ 2) for i in range(groups)]
    pair_a = [(i, (i + 1 if i % 2 else i - 1) % slabs) for i in range(slabs)]
    pair_b = [(i, i ^ 1) for i in range(slabs)]
    half = planes // 2
    plane = (depth, across)
    rest = planes - 2 * WIDE
    block = (chains, planes, *plane)
    rim_block = (chains, 2 * WIDE, *plane)
    inner_block = (chains, rest, *plane)
    halo = (2, chains, WIDE, *plane)
    edge = (chains * WIDE, *plane)
    sides = (2, *plane)
    tile = (chains, 8, LANES)
    scaled_shape = (chains, planes - 2, *plane)
    field = (chains, planes + 2 * WIDE, *plane)
    send_scratch = [rim_block, (2, chains, *plane)]
    inner_scratch = [block, scaled_shape]
    rim_scratch = [halo, field, rim_block, (chains, planes + 2, *plane)]
    work = chains * planes * depth * across * 30

    def swap(to_a, to_b):
        return lax.ppermute(to_a, "gx", pair_a), lax.ppermute(to_b, "gx", pair_b)

    first_edge = (chains * WIDE + 1, *plane)
    sums = (half, 2, *plane)
    position, keep, send, to_a, to_b = call(
        entry_kernel, [block, sums, sums, first_edge, first_edge],
        [(4, *plane), *send_scratch, pltpu.SemaphoreType.DMA((chains + 4,))], "entry", work // 16, [MEMORY] * 3,
    )(*(pltpu.with_memory_space_constraint(a, pltpu.HBM) for a in (position, viscosity, observed)))
    from_a, from_b = swap(to_a, to_b)
    got = lax.ppermute(send, "chain", near)

    def mass_body(*refs):
        mass_kernel(chains * groups, *refs)

    def mass_of(count, rim, after, before_mass, name):
        def add_body(*refs):
            add_kernel(rim, *refs)

        part = call(add_body, [(count, 2, *plane)], [], name + "_add", work // 16)(keep, got, *after)[0]
        remote = lax.ppermute(part, "chain", far)
        mine = call(mass_body, [(count, *plane)], [], name, work // 16)(part, remote, *before_mass)[0]
        return mine, lax.ppermute(mine, "chain", near)

    scaled, inner_slope, potential = call(
        first_inner_kernel, [scaled_shape, inner_block, tile], inner_scratch, "first_inner", work
    )(position, viscosity, observed)
    mine, other = mass_of(WIDE, True, (), (potential,), "mass_rim")
    slope, nu_halo, potential = call(
        first_rim_kernel, [rim_block, sides, tile], rim_scratch, "first_rim", work
    )(position, from_a, from_b, viscosity, observed, scaled, potential)
    inner_mine, inner_other = mass_of(half - WIDE, False, (slope,), (), "mass_inner")
    rim_q, rim_p, rim_mass, kinetic, to_a, to_b = call(
        launch_rim_kernel,
        [rim_block, rim_block, (2 * WIDE, *plane), tile, edge, edge],
        send_scratch, "launch_rim", work // 4,
    )(position, momentum_draw, slope, mine, other, viscosity, observed)
    from_a, from_b = swap(to_a, to_b)
    inner_q, inner_p, inner_mass, kinetic = call(
        launch_inner_kernel,
        [inner_block, inner_block, (rest, *plane), tile],
        [], "launch_inner", work // 4,
    )(position, momentum_draw, inner_slope, inner_mine, inner_other, kinetic)
    for _ in range(LEAPS - 1):
        old_rim, old_inner = rim_q, inner_q
        scaled, inner_q, inner_p = call(
            leap_inner_kernel, [scaled_shape, inner_block, inner_block], inner_scratch, "leap_inner", work
        )(old_rim, old_inner, viscosity, observed, inner_p, inner_mass)
        rim_q, rim_p, to_a, to_b = call(
            leap_rim_kernel, [rim_block, rim_block, edge, edge], rim_scratch + send_scratch, "leap_rim", work
        )(
            old_rim, old_inner, from_a, from_b, viscosity, observed, nu_halo,
            rim_p, rim_mass, scaled,
        )
        from_a, from_b = swap(to_a, to_b)
    copy_sems = pltpu.SemaphoreType.DMA((3 * chains,))
    q, stored = call(
        store_kernel, [block, (8, LANES)], [copy_sems], "store_q", work // 8, outs=[MEMORY, VECTOR]
    )(rim_q, inner_q)
    scaled, inner_p, energy = call(
        last_inner_kernel, [scaled_shape, inner_block, tile], inner_scratch, "last_inner", work
    )(rim_q, inner_q, viscosity, observed, inner_p, inner_mass)
    partial_p = call(
        store_inner_kernel, [block], [copy_sems], "store_p", work // 16, outs=[MEMORY]
    )(inner_p)[0]

    def last_body(*refs):
        last_rim_kernel(cells, *refs)

    operands = (
        rim_q, inner_q, from_a, from_b, viscosity, observed, nu_halo, rim_p, rim_mass,
        scaled, energy, potential, kinetic, stored, partial_p,
    )
    p, rows = call(
        last_body, [block, (slabs, 1, LANES)], [*rim_scratch, rim_block, copy_sems], "last_rim", work,
        [VECTOR] * (len(operands) - 1) + [MEMORY], [MEMORY, VECTOR], {len(operands) - 1: 0},
    )(*operands)
    rows = lax.all_to_all(rows, "gx", 0, 0, tiled=True)
    energies = jnp.sum(rows[:, 0, : 2 * chains].reshape(slabs, 2, chains), axis=0)
    return (q, p, energies)


def solution(mesh):
    in_specs = (
        P("chain", "gx", None, None),
        P("chain", "gx", None, None),
        P("gx", None, None),
        P("gx", None, None),
    )
    out_specs = (P("chain", "gx", None, None), P("chain", "gx", None, None), P(None, "chain"))
    return jax.shard_map(local, mesh=mesh, in_specs=in_specs, out_specs=out_specs, check_vma=False)
```

```python
import jax
import jax.numpy as jnp
from jax import lax
from jax.experimental import pallas as pl
from jax.experimental.pallas import tpu as pltpu
from jax.sharding import PartitionSpec as P

LEAPS = 2

unit = -0.05
inv_noise = 0.25
prior_weight = 0.5
step_size = 0.05
LANES = 128
WIDE = 2


VECTOR = pl.BlockSpec(memory_space=pltpu.VMEM)
MEMORY = pl.BlockSpec(memory_space=pltpu.HBM)


def call(kernel, out_shapes, scratch, name, work, ins=None, outs=None, aliases=None, limit=32):
    more = {} if ins is None else {"in_specs": ins}
    if aliases:
        more["input_output_aliases"] = aliases
    return pl.pallas_call(
        kernel,
        out_shape=[jax.ShapeDtypeStruct(shape, jnp.float32) for shape in out_shapes],
        out_specs=outs or [VECTOR] * len(out_shapes),
        scratch_shapes=[
            pltpu.VMEM(shape, jnp.float32) if isinstance(shape, tuple) else shape
            for shape in scratch
        ],
        compiler_params=pltpu.CompilerParams(vmem_limit_bytes=limit << 20),
        cost_estimate=pl.CostEstimate(flops=work, bytes_accessed=work // 8, transcendentals=0),
        name=name,
        **more,
    )


def tiles(width):
    return [slice(j * LANES, (j + 1) * LANES) for j in range(width // LANES)]


def depth_sum(v):
    depth = v.shape[0]
    row = lax.broadcasted_iota(jnp.int32, v.shape, 0)
    below = jnp.where(row == 0, 0.0, pltpu.roll(v, 1, 0))
    above = jnp.where(row == depth - 1, 0.0, pltpu.roll(v, depth - 1, 0))
    return below + above


def present(views, cut):
    value = None
    for view in views:
        if view is not None:
            value = view[:, cut] if value is None else value + view[:, cut]
    return value


def stencil(planes, deeps):
    cuts = tiles(planes[2].shape[-1])
    edge_terms, own_terms = [], []
    for cut in cuts:
        v = 0.0 if planes[1] is None else planes[1][:, cut]
        w = present([deeps[1], planes[0], planes[2]], cut)
        corner = present([deeps[0], deeps[2]], cut)
        t = 6.0 * v + (2.0 * w + corner)
        d = t + w
        edge_terms.append(t)
        own_terms.append((d + d) - 92.0 * v)
    lane = lax.broadcasted_iota(jnp.int32, edge_terms[0].shape, 1)
    ups = [pltpu.roll(t, 1, 1) for t in edge_terms]
    downs = [pltpu.roll(t, LANES - 1, 1) for t in edge_terms]
    result = []
    for j in range(len(cuts)):
        before = ups[j - 1] if j else 0.0
        after = downs[j + 1] if j + 1 < len(cuts) else 0.0
        left = jnp.where(lane == 0, before, ups[j])
        right = jnp.where(lane == LANES - 1, after, downs[j])
        result.append(own_terms[j] + (left + right))
    return list(zip(cuts, result, strict=True))


def deepen(deep, source):
    for cut in tiles(source.shape[-1]):
        deep[:, cut] = depth_sum(source[:, cut])


def weigh(view, deep, nu, target, out, out_deep):
    total = 0.0
    for cut, k in stencil(view, deep):
        n = nu[:, cut]
        misfit = (unit * n) * k - target[:, cut]
        s = n * misfit
        out[:, cut] = s
        out_deep[:, cut] = depth_sum(s)
        total = total + misfit * misfit
    return total


def fold(total):
    return total[:8] + total[8:]


def whole(q):
    return lambda chain, x: q.at[chain, x]


def parts(rim, inner):
    planes = inner.shape[1] + 2 * WIDE

    def at(chain, x):
        if x < WIDE:
            return rim.at[chain, x]
        if x >= planes - WIDE:
            return rim.at[chain, x - planes + 2 * WIDE]
        return inner.at[chain, x - WIDE]

    return at


def interior(q_at, nu, obs, scaled, deep, scaled_deep, use):
    chains, planes = deep.shape[:2]
    totals = []
    for chain in range(chains):
        for x in range(planes):
            deepen(deep.at[chain, x], q_at(chain, x))
    for chain in range(chains):
        total = 0.0
        for x in range(1, planes - 1):
            near = range(x - 1, x + 2)
            total = total + weigh(
                [q_at(chain, i) for i in near],
                [deep.at[chain, i] for i in near],
                nu.at[x],
                obs.at[x],
                scaled.at[chain, x - 1],
                scaled_deep.at[chain, x - 1],
            )
        totals.append(total)
    for chain in range(chains):
        for x in range(2, planes - 2):
            near = range(x - 2, x + 1)
            view = [scaled.at[chain, i] for i in near]
            for cut, k in stencil(view, [scaled_deep.at[chain, i] for i in near]):
                v = q_at(chain, x)[:, cut]
                use(chain, x, cut, v, (inv_noise * unit) * k + prior_weight * v)
    return totals


def parity():
    return 1 - lax.rem(lax.axis_index("gx"), 2)


def place_halo(halo, from_a, from_b):
    odd = parity()
    chains = halo.shape[1]
    for chain in range(chains):
        for i in range(WIDE):
            halo[1 - odd, chain, i] = from_a[chain * WIDE + i]
            halo[odd, chain, i] = from_b[chain * WIDE + i]


def rims(
    q_at, halo, nu, obs, nu_halo, scaled, deep, rim_scaled, scaled_deep, use, ready=None
):
    chains, planes = scaled.shape[0], scaled.shape[1] + 2

    def at(chain, x):
        if x < 0:
            return halo.at[0, chain, 0]
        if x >= planes:
            return halo.at[1, chain, 0]
        return q_at(chain, x)

    def scaled_at(chain, x):
        if x in (-1, 0):
            return rim_scaled.at[chain, x + 1]
        if x in (planes - 1, planes):
            return rim_scaled.at[chain, x - planes + 3]
        return scaled.at[chain, x - 1]

    sides = ((-1, 0, 1), (planes, planes - 1, planes - 2))
    totals = []
    for chain in range(chains):
        for side in sides:
            for x in side:
                deepen(deep.at[chain, x + WIDE], at(chain, x))
    for chain in range(chains):
        total = 0.0
        for s, (outer, x, _) in enumerate(sides):
            view = [None, None, at(chain, x)]
            for cut, k in stencil(view, [None, None, deep.at[chain, x + WIDE]]):
                n = nu_halo[s, :, cut]
                value = (unit * n * n) * k + halo[s, chain, 1, :, cut]
                scaled_at(chain, outer)[:, cut] = value
                scaled_deep[chain, outer + 1, :, cut] = depth_sum(value)
            near = range(x - 1, x + 2)
            total = total + weigh(
                [at(chain, i) for i in near],
                [deep.at[chain, i + WIDE] for i in near],
                nu.at[x],
                obs.at[x],
                scaled_at(chain, x),
                scaled_deep.at[chain, x + 1],
            )
            for x in (1, 2) if s == 0 else (planes - 2, planes - 3):
                deepen(scaled_deep.at[chain, x + 1], scaled_at(chain, x))
        totals.append(total)
    for chain in range(chains):
        for x in (0, 1, planes - 2, planes - 1):
            near = range(x - 1, x + 2)
            view = [scaled_at(chain, i) for i in near]
            for cut, k in stencil(view, [scaled_deep.at[chain, i + 1] for i in near]):
                v = q_at(chain, x)[:, cut]
                use(chain, x, cut, v, (inv_noise * unit) * k + prior_weight * v)
            if ready and x in (1, planes - 1):
                ready(chain, x > 1)
    return totals


def entry_kernel(q, nu, obs, own, keep, send, to_a, to_b, edges, deep, known, sems):
    core, odd = lax.rem(lax.axis_index("chain"), 2), parity()
    chains, planes = own.shape[:2]
    half = planes // 2
    load = [pltpu.make_async_copy(q.at[chain], own.at[chain], sems.at[chain]) for chain in range(chains)]
    for i, source in enumerate((nu, obs)):
        for side in range(2):
            at = 2 * i + side
            load.append(
                pltpu.make_async_copy(source.at[side * (planes - 1)], edges.at[at], sems.at[chains + at])
            )
    for copy in load:
        copy.start()
    for copy in load:
        copy.wait()
    near = (0, 1, planes - 2, planes - 1)
    send_rims(
        lambda chain, i: own.at[chain, near[i]],
        (edges.at[0], edges.at[1]), (edges.at[2], edges.at[3]), to_a, to_b, deep, known,
    )
    for chain in range(chains):
        to_a[2 * chain] = own[chain, (1 - odd) * (planes - 1)]
        to_b[2 * chain] = own[chain, odd * (planes - 1)]
    to_a[2 * chains] = edges[1 - odd]
    to_b[2 * chains] = edges[odd]
    for x in range(half):
        for out, base in ((keep, core * half), (send, (1 - core) * half)):
            for cut in tiles(own.shape[-1]):
                first = own[0, base + x, :, cut]
                second = first * first
                for chain in range(1, chains):
                    v = own[chain, base + x, :, cut]
                    first = first + v
                    second = second + v * v
                out[x, 0, :, cut] = first
                out[x, 1, :, cut] = second


def add_kernel(rim, a, b, *rest):
    core = lax.rem(lax.axis_index("chain"), 2)
    out = rest[-1]
    count = out.shape[0]
    for x in range(count):
        at = (core if rim else 1 - core) * count + x
        out[x] = a[at] + b[at]


def mass_kernel(count, a, b, *rest):
    out = rest[-1]
    for x in range(a.shape[0]):
        mean = (a[x, 0] + b[x, 0]) / count
        out[x] = 0.5 + (a[x, 1] + b[x, 1]) / count - mean * mean


def first_inner_kernel(q, nu, obs, scaled, slope, potential, deep, scaled_deep):
    chains, planes = q.shape[:2]

    def use(chain, x, cut, v, value):
        slope[chain, x - 2, :, cut] = value

    misfits = interior(whole(q), nu, obs, scaled, deep, scaled_deep, use)
    for chain in range(chains):
        squares = 0.0
        for x in range(planes):
            for cut in tiles(q.shape[-1]):
                v = q[chain, x, :, cut]
                squares = squares + v * v
        potential[chain] = fold(
            (0.5 * inv_noise) * misfits[chain] + (0.5 * prior_weight) * squares
        )


def first_rim_kernel(
    q, from_a, from_b, nu, obs, scaled, before,
    slope, nu_halo, potential, halo, deep, rim_scaled, scaled_deep,
):
    odd = parity()
    chains, planes = q.shape[:2]
    place_halo(halo, from_a, from_b)
    nu_halo[1 - odd] = from_a[chains * WIDE]
    nu_halo[odd] = from_b[chains * WIDE]

    def use(chain, x, cut, v, value):
        slope[chain, x if x < 2 else x - planes + 4, :, cut] = value

    misfits = rims(
        whole(q), halo, nu, obs, nu_halo, scaled, deep, rim_scaled, scaled_deep, use
    )
    for chain in range(chains):
        potential[chain] = before[chain] + fold((0.5 * inv_noise) * misfits[chain])


def launch(q, draw, slope, mine, other, base, new_q, new_p, mass, totals):
    chains = q.shape[0]
    for part, (start, offset) in ((mine, base[0]), (other, base[1])):
        for i in range(part.shape[0]):
            for cut in tiles(q.shape[-1]):
                im = part[i, :, cut]
                mass[offset + i, :, cut] = im
                inverse_root = 1.0 / jnp.sqrt(im)
                for chain in range(chains):
                    p = draw[chain, start + i, :, cut] * inverse_root
                    totals[chain] = totals[chain] + im * p * p
                    p = p - (0.5 * step_size) * slope[chain, offset + i, :, cut]
                    new_p[chain, offset + i, :, cut] = p
                    new_q[chain, offset + i, :, cut] = (
                        q[chain, start + i, :, cut] + step_size * im * p
                    )


def send_rims(rim, nu_edges, obs_edges, to_a, to_b, deep, known):
    odd = parity()
    chains = deep.shape[0]
    for chain in range(chains):
        for i in range(2 * WIDE):
            deepen(deep.at[chain, i], rim(chain, i))
        for side, (edge, inside) in enumerate(((0, 1), (3, 2))):
            view = [None, rim(chain, edge), rim(chain, inside)]
            for cut, k in stencil(view, [None, deep.at[chain, edge], deep.at[chain, inside]]):
                n = nu_edges[side][:, cut]
                known[side, chain, :, cut] = n * ((unit * n) * k - obs_edges[side][:, cut])
        to_a[2 * chain + 1] = known[1 - odd, chain]
        to_b[2 * chain + 1] = known[odd, chain]


def edges_of(field):
    return field.at[0], field.at[field.shape[0] - 1]


def send_new_rims(new_q, nu, obs, to_a, to_b, deep, known):
    odd = parity()
    send_rims(
        lambda chain, i: new_q.at[chain, i], edges_of(nu), edges_of(obs), to_a, to_b, deep, known
    )
    for chain in range(deep.shape[0]):
        to_a[2 * chain] = new_q[chain, (1 - odd) * 3]
        to_b[2 * chain] = new_q[chain, odd * 3]


def launch_rim_kernel(
    q, draw, slope, mine, other, nu, obs, new_q, new_p, mass, kinetic, to_a, to_b, deep, known
):
    core = lax.rem(lax.axis_index("chain"), 2)
    chains, planes = q.shape[:2]
    far = planes - WIDE
    totals = [0.0] * chains
    base = ((core * far, core * WIDE), ((1 - core) * far, (1 - core) * WIDE))
    launch(q, draw, slope, mine, other, base, new_q, new_p, mass, totals)
    for chain in range(chains):
        kinetic[chain] = fold(0.5 * totals[chain])
    send_new_rims(new_q, nu, obs, to_a, to_b, deep, known)


def launch_inner_kernel(q, draw, slope, mine, other, before, new_q, new_p, mass, kinetic):
    core = lax.rem(lax.axis_index("chain"), 2)
    chains, planes = q.shape[:2]
    half = planes // 2 - WIDE
    totals = [0.0] * chains
    base = tuple((WIDE + c * half, c * half) for c in (core, 1 - core))
    launch(q, draw, slope, mine, other, base, new_q, new_p, mass, totals)
    for chain in range(chains):
        kinetic[chain] = before[chain] + fold(0.5 * totals[chain])


def leap_inner_kernel(q_rim, q_inner, nu, obs, p, mass, scaled, new_q, new_p, deep, scaled_deep):
    def use(chain, x, cut, v, slope):
        at = x - WIDE
        moment = p[chain, at, :, cut] - step_size * slope
        new_p[chain, at, :, cut] = moment
        new_q[chain, at, :, cut] = v + step_size * mass[at, :, cut] * moment

    interior(parts(q_rim, q_inner), nu, obs, scaled, deep, scaled_deep, use)


def rim_index(x, planes):
    return x if x < WIDE else x - planes + 2 * WIDE


def leap_rim_kernel(
    q_rim, q_inner, from_a, from_b, nu, obs, nu_halo, p, mass, scaled,
    new_q, new_p, to_a, to_b, halo, deep, rim_scaled, scaled_deep, send_deep, known,
):
    planes = q_inner.shape[1] + 2 * WIDE
    place_halo(halo, from_a, from_b)

    def use(chain, x, cut, v, slope):
        at = rim_index(x, planes)
        moment = p[chain, at, :, cut] - step_size * slope
        new_p[chain, at, :, cut] = moment
        new_q[chain, at, :, cut] = v + step_size * mass[at, :, cut] * moment

    rims(
        parts(q_rim, q_inner), halo, nu, obs, nu_halo,
        scaled, deep, rim_scaled, scaled_deep, use,
    )
    send_new_rims(new_q, nu, obs, to_a, to_b, send_deep, known)


def run(copies):
    for copy in copies:
        copy.start()
    for copy in copies:
        copy.wait()


def rim_copies(rim, out, sems):
    chains, planes = out.shape[:2]
    copies = []
    for chain in range(chains):
        for side, start in enumerate((0, planes - WIDE)):
            copies.append(
                pltpu.make_async_copy(
                    rim.at[chain, pl.ds(side * WIDE, WIDE)],
                    out.at[chain, pl.ds(start, WIDE)],
                    sems.at[2 * chain + side],
                )
            )
    return copies


def inner_copies(inner, out, sems):
    chains, planes = out.shape[:2]
    return [
        pltpu.make_async_copy(
            inner.at[chain], out.at[chain, pl.ds(WIDE, planes - 2 * WIDE)], sems.at[2 * chains + chain]
        )
        for chain in range(chains)
    ]


def store_kernel(rim, inner, out, token, sems):
    token[...] = jnp.zeros_like(token)
    run(rim_copies(rim, out, sems) + inner_copies(inner, out, sems))


def store_inner_kernel(inner, out, sems):
    run(inner_copies(inner, out, sems))


def marked(tiles_of, row, cells, mark):
    lane = lax.broadcasted_iota(jnp.int32, mark.shape, 1)
    for chain, tile in enumerate(tiles_of):
        mark = jnp.where(lane == row * len(tiles_of) + chain, jnp.sum(tile) / cells, mark)
    return mark


def last_inner_kernel(
    cells, q_rim, q_inner, nu, obs, p, mass, potential, kinetic,
    scaled, new_p, energy, start, deep, scaled_deep,
):
    chains, planes = deep.shape[:2]
    q_at = parts(q_rim, q_inner)
    totals = [0.0] * chains

    def use(chain, x, cut, v, slope):
        at = x - WIDE
        moment = p[chain, at, :, cut] - (0.5 * step_size) * slope
        new_p[chain, at, :, cut] = moment
        totals[chain] = totals[chain] + (0.5 * mass[at, :, cut]) * (moment * moment)

    misfits = interior(q_at, nu, obs, scaled, deep, scaled_deep, use)
    for chain in range(chains):
        squares = 0.0
        for x in range(planes):
            view = q_at(chain, x)
            for cut in tiles(view.shape[-1]):
                v = view[:, cut]
                squares = squares + v * v
        energy[chain] = fold(
            (0.5 * inv_noise) * misfits[chain] + (0.5 * prior_weight) * squares + totals[chain]
        )
    tiles_of = [potential[chain] + kinetic[chain] for chain in range(chains)]
    start[...] = marked(tiles_of, 0, cells, jnp.zeros(start.shape, jnp.float32))


def last_rim_kernel(
    cells, q_rim, q_inner, from_a, from_b, nu, obs, nu_halo, p, mass, scaled, energy,
    start, stored,
    rim_p, rows, halo, deep, rim_scaled, scaled_deep,
):
    chains, planes = rim_p.shape[0], nu.shape[0]
    totals = [0.0] * chains
    place_halo(halo, from_a, from_b)

    def use(chain, x, cut, v, slope):
        at = rim_index(x, planes)
        moment = p[chain, at, :, cut] - (0.5 * step_size) * slope
        rim_p[chain, at, :, cut] = moment
        totals[chain] = totals[chain] + (0.5 * mass[at, :, cut]) * (moment * moment)

    misfits = rims(
        parts(q_rim, q_inner), halo, nu, obs, nu_halo,
        scaled, deep, rim_scaled, scaled_deep, use,
    )
    tiles_of = [
        energy[chain] + fold((0.5 * inv_noise) * misfits[chain] + totals[chain])
        for chain in range(chains)
    ]
    mark = marked(tiles_of, 1, cells, start[...])
    for i in range(rows.shape[0]):
        rows[i] = mark


def local(position, momentum_draw, viscosity, observed):
    chains, planes, depth, across = position.shape
    groups, slabs = lax.axis_size("chain"), lax.axis_size("gx")
    cells = planes * slabs * depth * across
    near = [(i, i ^ 1) for i in range(groups)]
    far = [(i, i ^ 2) for i in range(groups)]
    pair_a = [(i, (i + 1 if i % 2 else i - 1) % slabs) for i in range(slabs)]
    pair_b = [(i, i ^ 1) for i in range(slabs)]
    half = planes // 2
    plane = (depth, across)
    rest = planes - 2 * WIDE
    block = (chains, planes, *plane)
    rim_block = (chains, 2 * WIDE, *plane)
    inner_block = (chains, rest, *plane)
    halo = (2, chains, WIDE, *plane)
    edge = (chains * WIDE, *plane)
    sides = (2, *plane)
    tile = (chains, 8, LANES)
    scaled_shape = (chains, planes - 2, *plane)
    field = (chains, planes + 2 * WIDE, *plane)
    send_scratch = [rim_block, (2, chains, *plane)]
    inner_scratch = [block, scaled_shape]
    rim_scratch = [halo, field, rim_block, (chains, planes + 2, *plane)]
    work = chains * planes * depth * across * 30

    def swap(to_a, to_b):
        return lax.ppermute(to_a, "gx", pair_a), lax.ppermute(to_b, "gx", pair_b)

    first_edge = (chains * WIDE + 1, *plane)
    sums = (half, 2, *plane)
    position, keep, send, to_a, to_b = call(
        entry_kernel, [block, sums, sums, first_edge, first_edge],
        [(4, *plane), *send_scratch, pltpu.SemaphoreType.DMA((chains + 4,))], "entry", work // 16, [MEMORY] * 3,
    )(*(pltpu.with_memory_space_constraint(a, pltpu.HBM) for a in (position, viscosity, observed)))
    from_a, from_b = swap(to_a, to_b)
    got = lax.ppermute(send, "chain", near)

    def mass_body(*refs):
        mass_kernel(chains * groups, *refs)

    def mass_of(count, rim, after, before_mass, name):
        def add_body(*refs):
            add_kernel(rim, *refs)

        part = call(add_body, [(count, 2, *plane)], [], name + "_add", work // 16)(keep, got, *after)[0]
        remote = lax.ppermute(part, "chain", far)
        mine = call(mass_body, [(count, *plane)], [], name, work // 16)(part, remote, *before_mass)[0]
        return mine, lax.ppermute(mine, "chain", near)

    scaled, inner_slope, potential = call(
        first_inner_kernel, [scaled_shape, inner_block, tile], inner_scratch, "first_inner", work
    )(position, viscosity, observed)
    mine, other = mass_of(WIDE, True, (), (potential,), "mass_rim")
    slope, nu_halo, potential = call(
        first_rim_kernel, [rim_block, sides, tile], rim_scratch, "first_rim", work
    )(position, from_a, from_b, viscosity, observed, scaled, potential)
    inner_mine, inner_other = mass_of(half - WIDE, False, (slope,), (), "mass_inner")
    rim_q, rim_p, rim_mass, kinetic, to_a, to_b = call(
        launch_rim_kernel,
        [rim_block, rim_block, (2 * WIDE, *plane), tile, edge, edge],
        send_scratch, "launch_rim", work // 4,
    )(position, momentum_draw, slope, mine, other, viscosity, observed)
    from_a, from_b = swap(to_a, to_b)
    inner_q, inner_p, inner_mass, kinetic = call(
        launch_inner_kernel,
        [inner_block, inner_block, (rest, *plane), tile],
        [], "launch_inner", work // 4,
    )(position, momentum_draw, inner_slope, inner_mine, inner_other, kinetic)
    for _ in range(LEAPS - 1):
        old_rim, old_inner = rim_q, inner_q
        scaled, inner_q, inner_p = call(
            leap_inner_kernel, [scaled_shape, inner_block, inner_block], inner_scratch, "leap_inner", work
        )(old_rim, old_inner, viscosity, observed, inner_p, inner_mass)
        rim_q, rim_p, to_a, to_b = call(
            leap_rim_kernel, [rim_block, rim_block, edge, edge], rim_scratch + send_scratch, "leap_rim", work
        )(
            old_rim, old_inner, from_a, from_b, viscosity, observed, nu_halo,
            rim_p, rim_mass, scaled,
        )
        from_a, from_b = swap(to_a, to_b)
    copy_sems = pltpu.SemaphoreType.DMA((3 * chains,))
    q, stored = call(
        store_kernel, [block, (8, LANES)], [copy_sems], "store_q", work // 8, outs=[MEMORY, VECTOR]
    )(rim_q, inner_q)

    def last_inner_body(*refs):
        last_inner_kernel(cells, *refs)

    scaled, inner_p, energy, start = call(
        last_inner_body, [scaled_shape, inner_block, tile, (1, LANES)], inner_scratch, "last_inner", work
    )(rim_q, inner_q, viscosity, observed, inner_p, inner_mass, potential, kinetic)
    partial_p = call(
        store_inner_kernel, [block], [copy_sems], "store_p", work // 16, outs=[MEMORY]
    )(inner_p)[0]

    def last_body(*refs):
        last_rim_kernel(cells, *refs)

    operands = (
        rim_q, inner_q, from_a, from_b, viscosity, observed, nu_halo, rim_p, rim_mass,
        scaled, energy, start, stored,
    )
    rim_p, rows = call(
        last_body, [rim_block, (slabs, 1, LANES)], rim_scratch, "last_rim", work
    )(*operands)
    rows = lax.all_to_all(rows, "gx", 0, 0, tiled=True)

    def finish_kernel(rows, rim_p, partial_p, new_p, out, sems):
        copies = rim_copies(rim_p, new_p, sems)
        for copy in copies:
            copy.start()
        value = rows[0]
        for i in range(1, slabs):
            value = value + rows[i]
        for row in range(2):
            out[row : row + 1, :] = value[:, row * chains : (row + 1) * chains]
        for copy in copies:
            copy.wait()

    p, energies = call(
        finish_kernel, [block, (2, chains)], [copy_sems], "finish", work // 64,
        [VECTOR, VECTOR, MEMORY], [MEMORY, VECTOR], {2: 0},
    )(rows, rim_p, partial_p)
    return (q, p, energies)


def solution(mesh):
    in_specs = (
        P("chain", "gx", None, None),
        P("chain", "gx", None, None),
        P("gx", None, None),
        P("gx", None, None),
    )
    out_specs = (P("chain", "gx", None, None), P("chain", "gx", None, None), P(None, "chain"))
    return jax.shard_map(local, mesh=mesh, in_specs=in_specs, out_specs=out_specs, check_vma=False)
```
